32 devices in a mesh: section: 2 (over core), dp: 8 (over z, x), tensor: 2 (over y).
Axes of the slice: x: 2, y: 2, z: 4, core: 2. Of those that a mesh axis runs over, the one named last changes fastest.
Arguments:
- inputs: float32 [2048, 1024], P(('dp', 'tensor')), may hold values from -6 to 6
- segments: int32 [2048], P('dp'), may hold values from 0 to 1, never falling along the last dimension, each value on 1 to 1536 neighbouring positions
- mixer_gain: float32 [2, 1024], P('section', ('dp', 'tensor')), may hold values from 0.25 to 1.75
- query_weight: bfloat16 [2, 1024, 512], P('section', 'dp', 'tensor'), may hold values from -0.1875 to 0.1875
- key_weight: bfloat16 [2, 1024, 512], P('section', 'dp', 'tensor'), may hold values from -0.1875 to 0.1875
- value_weight: bfloat16 [2, 1024, 1024], P('section', 'dp', 'tensor'), may hold values from -0.1875 to 0.1875
- outgate_weight: bfloat16 [2, 1024, 1024], P('section', 'dp', 'tensor'), may hold values from -0.1875 to 0.1875
- decay_down: float32 [2, 1024, 16], P('section', ('dp', 'tensor')), may hold values from -0.1875 to 0.1875
- decay_up: float32 [2, 16, 512], P('section', None, ('dp', 'tensor')), may hold values from -1.5 to 1.5
- decay_bias: float32 [2, 512], P('section', ('dp', 'tensor')), may hold values from -3 to 7
- head_gain: float32 [2, 256], P('section', ('dp', 'tensor')), may hold values from 0.25 to 1.75
- output_weight: bfloat16 [2, 1024, 1024], P('section', 'tensor', 'dp'), may hold values from -0.1875 to 0.1875
- feed_gain: float32 [2, 1024], P('section', ('dp', 'tensor')), may hold values from 0.25 to 1.75
- gate_weight: bfloat16 [2, 1024, 2816], P('section', 'dp', 'tensor'), may hold values from -0.1875 to 0.1875
- up_weight: bfloat16 [2, 1024, 2816], P('section', 'dp', 'tensor'), may hold values from -0.1875 to 0.1875
- down_weight: bfloat16 [2, 2816, 1024], P('section', 'tensor', 'dp'), may hold values from -0.109375 to 0.109375
- cotangent: float32 [2048, 1024], P(('dp', 'tensor')), may hold values from -6 to 6
Outputs:
- section_outputs: float32 [2, 2048, 1024], P('section', ('dp', 'tensor'))
- input_grads: float32 [2, 2048, 1024], P('section', ('dp', 'tensor'))
- mixer_grad: float32 [2, 1024], P('section', ('dp', 'tensor'))
- query_grad: float32 [2, 1024, 512], P('section', 'dp', 'tensor')
- key_grad: float32 [2, 1024, 512], P('section', 'dp', 'tensor')
- value_grad: float32 [2, 1024, 1024], P('section', 'dp', 'tensor')
- outgate_grad: float32 [2, 1024, 1024], P('section', 'dp', 'tensor')
- downrank_grad: float32 [2, 1024, 16], P('section', ('dp', 'tensor'))
- uprank_grad: float32 [2, 16, 512], P('section', None, ('dp', 'tensor'))
- bias_grad: float32 [2, 512], P('section', ('dp', 'tensor'))
- headgain_grad: float32 [2, 256], P('section', ('dp', 'tensor'))
- output_grad: float32 [2, 1024, 1024], P('section', 'tensor', 'dp')
- feed_grad: float32 [2, 1024], P('section', ('dp', 'tensor'))
- gate_grad: float32 [2, 1024, 2816], P('section', 'dp', 'tensor')
- up_grad: float32 [2, 1024, 2816], P('section', 'dp', 'tensor')
- down_grad: float32 [2, 2816, 1024], P('section', 'tensor', 'dp')
The draws below stay inside these ranges and needn't reach their ends.
Inputs may be any that keep to these rules, and one draw needn't show every extreme that they name: `segments`: segment numbers never fall along the tokens; each of the 2 documents covers 1 to 1536 consecutive tokens,.
All inputs are finite; a program needn't handle non-finite values.
Results may differ from the reference program's by a relative error of at most 0.03.
Values may be sent and summed in bfloat16 or wider, within the bound.
No kernel may reach another device: no remote copies, remote signals or barrier semaphores. Data moves between devices by JAX's collectives and lax.ppermute only.
A program may use at most 128 MiB of HBM per device.

```python
import math
import jax
import jax.numpy as jnp
import numpy as np
from jax import lax

D = 1024
HEADS = 4
KDIM = 128
VDIM = 256
FF = 2816
RANK = 16
GROUP = 64
TOKENS = 2048
DOCS = 2
DOC_MAX = 1536
N_SECTION = 2


def shard_levels(rng, extent, split, low, high):
    def one(axis_at, parts):
        heights = jax.random.uniform(jax.random.fold_in(jax.random.fold_in(rng, 6), axis_at), (parts,), jnp.float32, low / len(split), high / len(split))
        return jnp.repeat(jnp.exp(heights), extent[axis_at] // parts).reshape((-1,) + (1,) * (len(extent) - axis_at - 1))

    loudness = one(*split[0])
    for cut in split[1:]:
        loudness = loudness * one(*cut)
    return loudness


def length_profile(count, total, most, skew):
    weights = [(1 << 20) // math.isqrt(standing ** skew) + 1 for standing in range(2, count + 1)]
    rest, counts = total - most - (count - 1), [1] * (count - 1)
    while rest > 0:
        candidates = [i for i in range(count - 1) if counts[i] < most]
        whole, budget = sum([weights[i] for i in candidates]), rest
        for i in candidates:
            addition = min(most - counts[i], max(1, budget * weights[i] // whole), rest)
            counts[i] = counts[i] + addition
            rest = rest - addition
    return np.array([most] + counts)


def ragged_sizes(own_key, number_of, total, bound, slope):
    if number_of == 2:
        one = jax.random.randint(own_key, (), max(1, total - bound), min(bound, total - 1) + 1)
        return jnp.stack([one, total - one])
    lengths = jnp.asarray(length_profile(number_of, total, bound, slope), jnp.int32)
    couples = (number_of - 1) // 2
    giver, sink = lengths[1:1 + 2 * couples:2], lengths[2:2 + 2 * couples:2]
    room = jnp.minimum(giver - 1, bound - sink)
    passed = jax.random.randint(jax.random.fold_in(own_key, 1), (couples,), 0, 1 << 20) % (room + 1)
    lengths = lengths.at[1:1 + 2 * couples:2].set(giver - passed).at[2:2 + 2 * couples:2].set(sink + passed)
    return lengths[jax.random.permutation(jax.random.fold_in(own_key, 2), number_of)]


def gaussian(stream_key, shape, spread, reach, cuts=(), dtype=jnp.bfloat16):
    values = spread * jax.random.normal(stream_key, shape, jnp.float32)
    if cuts:
        values = values * shard_levels(stream_key, shape, cuts, -0.22, 0.18)
    return jnp.clip(values, -reach, reach).astype(dtype)


def setup_inputs(seed: int = 0) -> dict:
    seeds = jax.random.split(jax.random.key(seed), 18)
    inputs = gaussian(seeds[0], (TOKENS, D), 1.0, 6.0, ((0, 16),), jnp.float32)
    segments = jnp.searchsorted(jnp.cumsum(ragged_sizes(seeds[1], DOCS, TOKENS, DOC_MAX, 1)), jnp.arange(TOKENS), side="right").astype(jnp.int32)
    mixer_gain = jnp.clip(1.0 + 0.15 * jax.random.normal(seeds[2], (N_SECTION, D), jnp.float32), 0.25, 1.75)
    query_weight = gaussian(seeds[3], (N_SECTION, D, HEADS * KDIM), D ** -0.5, 0.1875, ((0, 2), (1, 8), (2, 2)))
    key_weight = gaussian(seeds[4], (N_SECTION, D, HEADS * KDIM), D ** -0.5, 0.1875, ((0, 2), (1, 8), (2, 2)))
    value_weight = gaussian(seeds[5], (N_SECTION, D, HEADS * VDIM), D ** -0.5, 0.1875, ((0, 2), (1, 8), (2, 2)))
    outgate_weight = gaussian(seeds[6], (N_SECTION, D, HEADS * VDIM), D ** -0.5, 0.1875, ((0, 2), (1, 8), (2, 2)))
    decay_down = gaussian(seeds[7], (N_SECTION, D, RANK), D ** -0.5, 0.1875, ((0, 2), (1, 16)), jnp.float32)
    decay_up = gaussian(seeds[8], (N_SECTION, RANK, HEADS * KDIM), RANK ** -0.5, 1.5, ((0, 2), (2, 16)), jnp.float32)
    decay_bias = jnp.clip(-3.0 + 10.0 * jax.random.uniform(seeds[9], (N_SECTION, HEADS * KDIM), jnp.float32) ** shard_levels(seeds[9], (N_SECTION, HEADS * KDIM), ((0, 2), (1, 16)), -0.2, 0.2), -3.0, 7.0)
    head_gain = jnp.clip(1.0 + 0.15 * jax.random.normal(seeds[10], (N_SECTION, VDIM), jnp.float32), 0.25, 1.75)
    output_weight = gaussian(seeds[11], (N_SECTION, HEADS * VDIM, D), (HEADS * VDIM) ** -0.5, 0.1875, ((0, 2), (1, 2), (2, 8)))
    feed_gain = jnp.clip(1.0 + 0.15 * jax.random.normal(seeds[12], (N_SECTION, D), jnp.float32), 0.25, 1.75)
    gate_weight = gaussian(seeds[13], (N_SECTION, D, FF), D ** -0.5, 0.1875, ((0, 2), (1, 8), (2, 2)))
    up_weight = gaussian(seeds[14], (N_SECTION, D, FF), D ** -0.5, 0.1875, ((0, 2), (1, 8), (2, 2)))
    down_weight = gaussian(seeds[15], (N_SECTION, FF, D), FF ** -0.5, 0.109375, ((0, 2), (1, 2), (2, 8)))
    cotangent = gaussian(seeds[16], (TOKENS, D), 1.0, 6.0, ((0, 16),), jnp.float32)
    return {"inputs": inputs, "segments": segments, "mixer_gain": mixer_gain, "query_weight": query_weight, "key_weight": key_weight, "value_weight": value_weight, "outgate_weight": outgate_weight, "decay_down": decay_down, "decay_up": decay_up, "decay_bias": decay_bias, "head_gain": head_gain, "output_weight": output_weight, "feed_gain": feed_gain, "gate_weight": gate_weight, "up_weight": up_weight, "down_weight": down_weight, "cotangent": cotangent}


exact_mode = lax.Precision.HIGHEST
norm_eps = 1e-06
head_eps = 1e-05

def product(left, right):
    return jnp.dot(left, right, preferred_element_type=jnp.float32)

def exact_product(left, right):
    return jnp.dot(left, right, precision=exact_mode, preferred_element_type=jnp.float32)

def rms_scale(values, epsilon):
    return lax.rsqrt(lax.optimization_barrier(jnp.mean(values * values, axis=-1, keepdims=True)) + epsilon)

def to_heads(values, column_count):
    token_count = values.shape[0]
    return values.reshape(token_count, -1, column_count).transpose(1, 0, 2)

def from_heads(values):
    head_count, token_count, column_count = values.shape
    return values.transpose(1, 0, 2).reshape(token_count, head_count * column_count)

def norm_back(grad_unit, unit_values, scale_values):
    return scale_values * (grad_unit - unit_values * lax.optimization_barrier(jnp.mean(grad_unit * unit_values, axis=-1, keepdims=True)))

def silu_slope(values):
    sigma = jax.nn.sigmoid(values)
    return sigma * (1.0 + values * (1.0 - sigma))

def gla_groups(query_heads, key_heads, value_heads, decay_heads, segment_ids, state_start, segment_before):
    head_count, token_count, key_width = query_heads.shape
    value_width = value_heads.shape[2]
    block_count = token_count // GROUP

    def to_blocks(tensor):
        return tensor.reshape(head_count, block_count, GROUP, tensor.shape[2]).transpose(1, 0, 2, 3)
    positions = jnp.arange(GROUP)
    causal = positions[:, None] >= positions[None, :]

    def advance(running, pieces):
        state_now, segment_prev = running
        query_block, key_block, value_block, decay_block, segment_block = pieces
        decay_sums = jnp.cumsum(decay_block, axis=1)
        allowed = causal & (segment_block[:, None] == segment_block[None, :])
        allowed_full = allowed[None, :, :, None]
        spans = decay_sums[:, :, None, :] - decay_sums[:, None, :, :]
        factors = jnp.where(allowed_full, jnp.exp(jnp.where(allowed_full, spans, 0.0)), 0.0)
        scores = lax.optimization_barrier(jnp.sum(query_block[:, :, None, :] * key_block[:, None, :, :] * factors, axis=-1))
        within = jnp.einsum('hts,hse->hte', scores, value_block, precision=exact_mode)
        carried = jnp.where((segment_block == segment_prev)[None, :, None], query_block * jnp.exp(decay_sums), 0.0)
        across = jnp.einsum('htd,hde->hte', carried, state_now, precision=exact_mode)
        block_end = decay_sums[:, GROUP - 1:, :]
        segment_end = segment_block[GROUP - 1]
        kept_keys = jnp.where((segment_block == segment_end)[None, :, None], key_block * jnp.exp(block_end - decay_sums), 0.0)
        factor = jnp.where(segment_end == segment_prev, jnp.exp(block_end[:, 0, :]), 0.0)
        state_next = factor[:, :, None] * state_now + jnp.einsum('hsd,hse->hde', kept_keys, value_block, precision=exact_mode)
        return ((state_next, segment_end), within + across)
    pieces = (to_blocks(query_heads), to_blocks(key_heads), to_blocks(value_heads), to_blocks(decay_heads), segment_ids.reshape(block_count, GROUP))
    (state_end, _), outputs = lax.scan(jax.checkpoint(advance), (state_start, segment_before), pieces)
    return (outputs.transpose(1, 0, 2, 3).reshape(head_count, token_count, value_width), state_end)

def layer_forward(layer_in, segment_ids, params):
    mixer_gain, query_weight, key_weight, value_weight, outgate_weight, decay_down, decay_up, decay_bias, head_gain, output_weight, feed_gain, gate_weight, up_weight, down_weight = params
    scale_one = rms_scale(layer_in, norm_eps)
    hidden_one = (layer_in * scale_one * mixer_gain).astype(jnp.bfloat16)
    query_heads = to_heads(product(hidden_one, query_weight), KDIM)
    key_heads = to_heads(product(hidden_one, key_weight), KDIM)
    value_heads = to_heads(product(hidden_one, value_weight), VDIM)
    outgate_heads = to_heads(product(hidden_one, outgate_weight), VDIM)
    latent = exact_product(hidden_one.astype(jnp.float32), decay_down)
    logits = exact_product(latent, decay_up) + decay_bias
    decay_heads = to_heads(jax.nn.log_sigmoid(logits) / 16.0, KDIM)
    start_state = jnp.zeros((query_heads.shape[0], KDIM, VDIM), jnp.float32)
    before = jnp.asarray(-1.0, jnp.float32)
    mixed_heads, _ = gla_groups(query_heads, key_heads, value_heads, decay_heads, segment_ids, start_state, before)
    scale_head = rms_scale(mixed_heads, head_eps)
    unit_head = mixed_heads * scale_head
    branch = from_heads(unit_head * head_gain * jax.nn.silu(outgate_heads)).astype(jnp.bfloat16)
    mid_stream = layer_in + product(branch, output_weight)
    scale_two = rms_scale(mid_stream, norm_eps)
    hidden_two = (mid_stream * scale_two * feed_gain).astype(jnp.bfloat16)
    gate_pre = product(hidden_two, gate_weight)
    up_pre = product(hidden_two, up_weight)
    inner_act = (jax.nn.silu(gate_pre) * up_pre).astype(jnp.bfloat16)
    result = mid_stream + product(inner_act, down_weight)
    saved = (layer_in, scale_one, hidden_one, query_heads, key_heads, value_heads, decay_heads, outgate_heads, latent, logits, scale_head, unit_head, branch, mid_stream, scale_two, hidden_two, gate_pre, up_pre, inner_act)
    return (result, saved)

def layer_backward(saved, cotangent_in, segment_ids, params):
    mixer_gain, query_weight, key_weight, value_weight, outgate_weight, decay_down, decay_up, decay_bias, head_gain, output_weight, feed_gain, gate_weight, up_weight, down_weight = params
    layer_in, scale_one, hidden_one, query_heads, key_heads, value_heads, decay_heads, outgate_heads, latent, logits, scale_head, unit_head, branch, mid_stream, scale_two, hidden_two, gate_pre, up_pre, inner_act = saved
    cot_low = cotangent_in.astype(jnp.bfloat16)
    inner_delta = product(cot_low, down_weight.T)
    down_grad = product(inner_act.T, cot_low)
    gate_delta = (inner_delta * up_pre * silu_slope(gate_pre)).astype(jnp.bfloat16)
    up_delta = (inner_delta * jax.nn.silu(gate_pre)).astype(jnp.bfloat16)
    hidden_two_delta = product(gate_delta, gate_weight.T) + product(up_delta, up_weight.T)
    gate_grad = product(hidden_two.T, gate_delta)
    up_grad = product(hidden_two.T, up_delta)
    unit_two = mid_stream * scale_two
    feed_grad = lax.optimization_barrier(jnp.sum(hidden_two_delta * unit_two, axis=0))
    mid_delta = cotangent_in + norm_back(hidden_two_delta * feed_gain, unit_two, scale_two)
    mid_low = mid_delta.astype(jnp.bfloat16)
    branch_delta = to_heads(product(mid_low, output_weight.T), VDIM)
    output_grad = product(branch.T, mid_low)
    swish = jax.nn.silu(outgate_heads)
    unit_delta = branch_delta * swish * head_gain
    outgate_delta = branch_delta * unit_head * head_gain * silu_slope(outgate_heads)
    headgain_grad = lax.optimization_barrier(jnp.sum(branch_delta * swish * unit_head, axis=(0, 1)))
    mixed_delta = norm_back(unit_delta, unit_head, scale_head)
    start_state = jnp.zeros((query_heads.shape[0], KDIM, VDIM), jnp.float32)
    before = jnp.asarray(-1.0, jnp.float32)

    def recurrence(query_part, key_part, value_part, decay_part):
        return gla_groups(query_part, key_part, value_part, decay_part, segment_ids, start_state, before)[0]
    _, pull_back = jax.vjp(recurrence, query_heads, key_heads, value_heads, decay_heads)
    query_delta, key_delta, value_delta, decay_delta = pull_back(mixed_delta)
    logit_delta = from_heads(decay_delta) * jax.nn.sigmoid(-logits) / 16.0
    bias_grad = lax.optimization_barrier(jnp.sum(logit_delta, axis=0))
    uprank_grad = exact_product(latent.T, logit_delta)
    latent_delta = exact_product(logit_delta, decay_up.T)
    query_low = from_heads(query_delta).astype(jnp.bfloat16)
    key_low = from_heads(key_delta).astype(jnp.bfloat16)
    value_low = from_heads(value_delta).astype(jnp.bfloat16)
    outgate_low = from_heads(outgate_delta).astype(jnp.bfloat16)
    hidden_one_delta = product(query_low, query_weight.T) + product(key_low, key_weight.T) + product(value_low, value_weight.T) + product(outgate_low, outgate_weight.T) + exact_product(latent_delta, decay_down.T)
    query_grad = product(hidden_one.T, query_low)
    key_grad = product(hidden_one.T, key_low)
    value_grad = product(hidden_one.T, value_low)
    outgate_grad = product(hidden_one.T, outgate_low)
    downrank_grad = exact_product(hidden_one.astype(jnp.float32).T, latent_delta)
    unit_one = layer_in * scale_one
    mixer_grad = lax.optimization_barrier(jnp.sum(hidden_one_delta * unit_one, axis=0))
    input_delta = mid_delta + norm_back(hidden_one_delta * mixer_gain, unit_one, scale_one)
    grads = (mixer_grad, query_grad, key_grad, value_grad, outgate_grad, downrank_grad, uprank_grad, bias_grad, headgain_grad, output_grad, feed_grad, gate_grad, up_grad, down_grad)
    return (input_delta, grads)

def reference(inputs, segments, mixer_gain, query_weight, key_weight, value_weight, outgate_weight, decay_down, decay_up, decay_bias, head_gain, output_weight, feed_gain, gate_weight, up_weight, down_weight, cotangent):
    segment_ids = segments.astype(jnp.float32)
    stacks = (mixer_gain, query_weight, key_weight, value_weight, outgate_weight, decay_down, decay_up, decay_bias, head_gain, output_weight, feed_gain, gate_weight, up_weight, down_weight)
    first_params = tuple((weight_stack[0] for weight_stack in stacks))
    second_params = tuple((weight_stack[1] for weight_stack in stacks))
    first_out, first_saved = layer_forward(inputs, segment_ids, first_params)
    second_out, second_saved = layer_forward(first_out, segment_ids, second_params)
    between_grad, second_grads = layer_backward(second_saved, cotangent, segment_ids, second_params)
    input_grad, first_grads = layer_backward(first_saved, between_grad, segment_ids, first_params)

    def stacked_grad(position):
        return jnp.stack([first_grads[position], second_grads[position]])
    return (jnp.stack([first_out, second_out]), jnp.stack([input_grad, between_grad]), stacked_grad(0), stacked_grad(1), stacked_grad(2), stacked_grad(3), stacked_grad(4), stacked_grad(5), stacked_grad(6), stacked_grad(7), stacked_grad(8), stacked_grad(9), stacked_grad(10), stacked_grad(11), stacked_grad(12), stacked_grad(13))
```

```python
import functools

import jax
import jax.numpy as jnp
from jax import lax
from jax.experimental import pallas as pl
from jax.experimental.pallas import tpu as pltpu
from jax.sharding import PartitionSpec as P

HEADS = 4
KDIM = 128
VDIM = 256
RANK = 16
SUB = 16
PACK = 128
STATE_PAD = 16

norm_eps = 1e-06
head_eps = 1e-05
f32 = jnp.float32
bf16 = jnp.bfloat16
INTERPRET = False


def swap(block, axis):
    return lax.ppermute(block, axis, [(0, 1), (1, 0)])


def mm(left, right, dims):
    return lax.dot_general(left, right, (dims, ((), ())), preferred_element_type=f32)


def exact(left, right, dims=((1,), (0,))):
    return lax.dot_general(
        left, right, (dims, ((), ())), precision=lax.Precision.HIGHEST, preferred_element_type=f32
    )


NN = ((1,), (0,))
NT = ((1,), (1,))
TN = ((0,), (0,))


def call(body, outs, *args):
    return pl.pallas_call(
        body,
        out_shape=[jax.ShapeDtypeStruct(shape, kind) for shape, kind in outs],
        interpret=INTERPRET,
    )(*args)


def iota2(rows, cols, axis):
    return lax.broadcasted_iota(jnp.int32, (rows, cols), axis)


def lower(count):
    return jnp.where(iota2(count, count, 0) >= iota2(count, count, 1), 1.0, 0.0)


def levels(count):
    half, out = count // 2, []
    while half >= SUB:
        out.append(half)
        half //= 2
    return out


def level_factors(sums, half):
    count, width = sums.shape
    parts = sums.reshape(count // (2 * half), 2 * half, width)
    middle = jnp.broadcast_to(parts[:, half - 1 : half, :], parts.shape).reshape(count, width)
    late = (iota2(count, width, 0) & half) != 0
    gap = sums - middle
    to_late = jnp.where(late, jnp.exp(jnp.minimum(gap, 0.0)), 0.0)
    to_early = jnp.where(late, 0.0, jnp.exp(jnp.minimum(-gap, 0.0)))
    return to_late, to_early


def level_mask(count, half):
    rows, cols = iota2(count, count, 0), iota2(count, count, 1)
    bits = 2 * half - 1
    return (rows & ~bits) == (cols & ~bits)


def pair_mask(seg_col, seg_row, count):
    same = seg_col == seg_row
    return same & (iota2(count, count, 0) >= iota2(count, count, 1))


def pick_mask(count, offset):
    rows, cols = iota2(count, count, 0), iota2(count, count, 1)
    return cols == ((rows & ~(SUB - 1)) + offset)


def sub_factor(sums3, offset):
    return jnp.exp(jnp.minimum(sums3 - sums3[:, offset : offset + 1, :], 0.0))


def pre_body(
    proj, up3, bias, seg_col, seg_before, logits_o, sums_o, open_o, keep_o, end_o, through_o, pack_o
):
    count = proj.shape[0]
    logits = exact(proj[:, 768:896], up3[...]) + bias[...]
    decay = (jnp.minimum(logits, 0.0) - jnp.log1p(jnp.exp(-jnp.abs(logits)))) / 16.0
    sums = exact(lower(count), decay)
    last = sums[count - 1 : count, :]
    seg = seg_col[...]
    seg_last = seg[count - 1 : count, :]
    before = seg_before[...]
    opened = jnp.where(seg == before, proj[:, 0:128] * jnp.exp(sums), 0.0)
    kept = jnp.where(seg == seg_last, proj[:, 128:256] * jnp.exp(last - sums), 0.0)
    state = exact(proj[:, 256:512], kept, TN)
    through = jnp.where(before == seg_last, jnp.exp(last), 0.0)
    logits_o[...] = logits
    sums_o[...] = sums
    open_o[...] = opened
    keep_o[...] = kept
    end_o[...] = state
    through_o[...] = through
    pack_o[0:VDIM, :] = state.astype(bf16)
    pack_o[VDIM : VDIM + STATE_PAD, :] = jnp.broadcast_to(through, (STATE_PAD, KDIM)).astype(bf16)


def within_body(proj, sums_r, seg_col, seg_row, scores_o, out_o):
    count = proj.shape[0]
    query, key = proj[:, 0:128], proj[:, 128:256]
    sums = sums_r[...]
    scores = jnp.zeros((count, count), f32)
    for half in levels(count):
        to_late, to_early = level_factors(sums, half)
        part = exact(query * to_late, key * to_early, NT)
        scores = scores + jnp.where(level_mask(count, half), part, 0.0)
    blocks = (count // SUB, SUB, KDIM)
    query3, key3, sums3 = query.reshape(blocks), key.reshape(blocks), sums.reshape(blocks)
    for offset in range(SUB):
        weight = sub_factor(sums3, offset)
        column = jnp.sum(query3 * weight * key3[:, offset : offset + 1, :], axis=-1, keepdims=True)
        scores = jnp.where(pick_mask(count, offset), column.reshape(count, 1), scores)
    scores = jnp.where(pair_mask(seg_col[...], seg_row[...], count), scores, 0.0)
    scores_o[...] = scores
    out_o[...] = exact(scores, proj[:, 256:512])


def post_body(within, opened, state_in, proj, gain, unit_o, scale_o, branch_o):
    mixed = within[...] + exact(opened[...], state_in[...], NT)
    scale = lax.rsqrt(jnp.mean(mixed * mixed, axis=-1, keepdims=True) + head_eps)
    unit = mixed * scale
    gate = proj[:, 512:768]
    unit_o[...] = unit
    scale_o[...] = scale
    branch_o[...] = (unit * gain[...] * (gate * jax.nn.sigmoid(gate))).astype(bf16)


def head_back_body(
    branch_delta, unit_r, scale, proj, gain_r, opened, through, low_o, gain_o, mixed_o, pack_o
):
    delta, unit, gate, gain = branch_delta[...], unit_r[...], proj[:, 512:768], gain_r[...]
    sigma = jax.nn.sigmoid(gate)
    swish = gate * sigma
    slope = sigma * (1.0 + gate * (1.0 - sigma))
    low_o[...] = (delta * unit * gain * slope).astype(bf16)
    through_unit = delta * swish
    gain_o[...] = jnp.sum(through_unit * unit, axis=0, keepdims=True)
    inner = through_unit * gain
    mixed = scale[...] * (inner - unit * jnp.mean(inner * unit, axis=-1, keepdims=True))
    mixed_o[...] = mixed
    pack_o[0:VDIM, :] = exact(mixed, opened[...], TN).astype(bf16)
    pack_o[VDIM : VDIM + STATE_PAD, :] = jnp.broadcast_to(
        through[...], (STATE_PAD, KDIM)
    ).astype(bf16)


def within_back_body(
    mixed_r, proj, sums_r, scores, seg_col, seg_row, seg_before, state_in, query_o, key_o, value_o
):
    count = proj.shape[0]
    query, key, value = proj[:, 0:128], proj[:, 128:256], proj[:, 256:512]
    sums, mixed = sums_r[...], mixed_r[...]
    value_o[...] = exact(scores[...], mixed, TN)
    grad = jnp.where(
        pair_mask(seg_col[...], seg_row[...], count), exact(mixed, value, NT), 0.0
    )
    query_delta = jnp.where(
        seg_col[...] == seg_before[...], jnp.exp(sums) * exact(mixed, state_in[...]), 0.0
    )
    key_delta = jnp.zeros((count, KDIM), f32)
    for half in levels(count):
        to_late, to_early = level_factors(sums, half)
        part = jnp.where(level_mask(count, half), grad, 0.0)
        query_delta = query_delta + to_late * exact(part, key * to_early)
        key_delta = key_delta + to_early * exact(part, query * to_late, TN)
    blocks = (count // SUB, SUB, KDIM)
    query3, key3, sums3 = query.reshape(blocks), key.reshape(blocks), sums.reshape(blocks)
    place = lax.broadcasted_iota(jnp.int32, blocks, 1)
    query_sub, key_sub = jnp.zeros(blocks, f32), jnp.zeros(blocks, f32)
    for offset in range(SUB):
        weight = sub_factor(sums3, offset)
        column = jnp.sum(jnp.where(pick_mask(count, offset), grad, 0.0), axis=-1, keepdims=True)
        weighted = weight * column.reshape(count // SUB, SUB, 1)
        query_sub = query_sub + weighted * key3[:, offset : offset + 1, :]
        total = jnp.sum(weighted * query3, axis=1, keepdims=True)
        key_sub = jnp.where(place == offset, total, key_sub)
    query_o[...] = query_delta + query_sub.reshape(count, KDIM)
    key_o[...] = key_delta + key_sub.reshape(count, KDIM)


def state_back_body(
    query_d, key_d, value_d, state_grad, state_in, state_end, through, proj, sums_r, kept,
    logits, seg_col, up3, gate_low, low_o, up_o, bias_o,
):
    count = proj.shape[0]
    grad, sums = state_grad[...], sums_r[...]
    last = sums[count - 1 : count, :]
    seg = seg_col[...]
    query_delta = query_d[...]
    value_delta = value_d[...] + exact(kept[...], grad, NT)
    key_delta = key_d[...] + jnp.where(
        seg == seg[count - 1 : count, :],
        jnp.exp(last - sums) * exact(proj[:, 256:512], grad),
        0.0,
    )
    final = state_end[...] + through[...] * state_in[...]
    beyond = jnp.sum(final * grad, axis=0, keepdims=True)
    local = proj[:, 0:128] * query_delta - proj[:, 128:256] * key_delta
    decay_delta = exact(lower(count), local, TN) + beyond
    logit_delta = decay_delta * jax.nn.sigmoid(-logits[...]) / 16.0
    bias_o[...] = jnp.sum(logit_delta, axis=0, keepdims=True)
    ranks = exact(proj[:, 768:896], logit_delta, TN)
    up_o[...] = ranks[0:16, :] + ranks[16:32, :] + ranks[32:48, :]
    low_o[:, 0:128] = query_delta.astype(bf16)
    low_o[:, 128:256] = key_delta.astype(bf16)
    low_o[:, 256:512] = value_delta.astype(bf16)
    low_o[:, 512:768] = gate_low[...]
    low_o[:, 768:896] = exact(logit_delta, up3[...], NT).astype(bf16)


def scan_states(pack, backward):
    count = lax.axis_size("dp")
    here = lax.axis_index("dp")
    state = pack[:VDIM].astype(f32)
    through = pack[VDIM : VDIM + 1].astype(f32)
    carried, passed = jnp.zeros_like(state), jnp.ones_like(through)
    step = 1
    while step < count:
        other = lax.ppermute(pack, "dp", [(i, i ^ step) for i in range(count)])
        other_state = other[:VDIM].astype(f32)
        other_through = other[VDIM : VDIM + 1].astype(f32)
        mine_later = (here & step) != 0
        ahead = jnp.logical_not(mine_later) if backward else mine_later
        carried = jnp.where(ahead, carried + passed * other_state, carried)
        passed = jnp.where(ahead, passed * other_through, passed)
        state = jnp.where(ahead, state + through * other_state, other_state + other_through * state)
        through = through * other_through
        step *= 2
        if step < count:
            pack = jnp.concatenate(
                [state, jnp.broadcast_to(through, (STATE_PAD, KDIM))], axis=0
            ).astype(bf16)
    return carried


def gather_tokens(block, tensor_index, section_index):
    other = swap(block, "tensor")
    first = tensor_index == 0
    pair = jnp.stack([jnp.where(first, block, other), jnp.where(first, other, block)])
    far = swap(pair, "section")
    left = section_index == 0
    whole = jnp.stack([jnp.where(left, pair, far), jnp.where(left, far, pair)], axis=1)
    return whole.reshape(4 * block.shape[0], block.shape[1])


def scatter_tokens(partial, kind, tensor_index, section_index):
    rows = partial.shape[0] // 4
    parts = partial.reshape(2, 2, rows, partial.shape[1])
    left = section_index == 0
    keep = jnp.where(left, parts[:, 0], parts[:, 1])
    send = jnp.where(left, parts[:, 1], parts[:, 0])
    both = keep + swap(send, "section")
    first = tensor_index == 0
    mine = jnp.where(first, both[0], both[1])
    theirs = jnp.where(first, both[1], both[0]).astype(kind)
    return mine + swap(theirs, "tensor").astype(f32)


def rms_scale(values, epsilon):
    return lax.rsqrt(jnp.mean(values * values, axis=-1, keepdims=True) + epsilon)


def norm_back(grad_unit, unit_values, scale_values):
    return scale_values * (
        grad_unit - unit_values * jnp.mean(grad_unit * unit_values, axis=-1, keepdims=True)
    )


def layer_forward(layer_in, seg, params, where):
    attn, feed, small = params
    mixer_gain, feed_gain, up3, bias, head_gain = small
    seg_col, seg_row, seg_before = seg
    count = seg_col.shape[0]
    scale_one = rms_scale(layer_in, norm_eps)
    hidden_one = gather_tokens((layer_in * scale_one * mixer_gain).astype(bf16), *where)
    proj = mm(hidden_one, attn[:, :896], NN)
    wide, tall = (count, KDIM), (count, VDIM)
    logits, sums, opened, kept, state_end, through, pack = call(
        pre_body,
        [(wide, f32)] * 4
        + [((VDIM, KDIM), f32), ((1, KDIM), f32), ((VDIM + STATE_PAD, KDIM), bf16)],
        proj, up3, bias, seg_col, seg_before,
    )
    scores, within = call(
        within_body, [((count, count), f32), (tall, f32)], proj, sums, seg_col, seg_row
    )
    state_in = scan_states(pack, False)
    unit, scale_head, branch = call(
        post_body,
        [(tall, f32), ((count, 1), f32), (tall, bf16)],
        within, opened, state_in, proj, head_gain,
    )
    mid = layer_in + scatter_tokens(mm(branch, attn[:, 896:], NT), f32, *where)
    scale_two = rms_scale(mid, norm_eps)
    hidden_two = gather_tokens((mid * scale_two * feed_gain).astype(bf16), *where)
    units = feed.shape[1] // 3
    both = mm(hidden_two, feed[:, : 2 * units], NN)
    gate_pre, up_pre = both[:, :units], both[:, units:]
    inner = (jax.nn.silu(gate_pre) * up_pre).astype(bf16)
    result = mid + scatter_tokens(mm(inner, feed[:, 2 * units :], NT), f32, *where)
    saved = (
        layer_in, scale_one, hidden_one, proj, logits, sums, opened, kept, state_end, through,
        scores, state_in, unit, scale_head, branch, mid, scale_two, hidden_two, both, inner,
    )
    return result, saved


def layer_backward(saved, cotangent, seg, params, where):
    attn, feed, small = params
    mixer_gain, feed_gain, up3, bias, head_gain = small
    seg_col, seg_row, seg_before = seg
    (
        layer_in, scale_one, hidden_one, proj, logits, sums, opened, kept, state_end, through,
        scores, state_in, unit, scale_head, branch, mid, scale_two, hidden_two, both, inner,
    ) = saved
    count = seg_col.shape[0]
    wide, tall = (count, KDIM), (count, VDIM)
    units = feed.shape[1] // 3
    cot = gather_tokens(cotangent.astype(bf16), *where)
    inner_delta = mm(cot, feed[:, 2 * units :], NN)
    gate_pre, up_pre = both[:, :units], both[:, units:]
    sigma = jax.nn.sigmoid(gate_pre)
    gate_delta = inner_delta * up_pre * (sigma * (1.0 + gate_pre * (1.0 - sigma)))
    up_delta = inner_delta * (gate_pre * sigma)
    low_two = jnp.concatenate([gate_delta, up_delta], axis=1).astype(bf16)
    two_delta = mm(low_two, feed[:, : 2 * units], NT)
    feed_grad = jnp.concatenate(
        [mm(hidden_two, low_two, TN).astype(bf16), mm(cot, inner, TN).astype(bf16)], axis=1
    )
    feed_reduced = lax.psum_scatter(feed_grad, "dp", scatter_dimension=0, tiled=True)
    feed_gain_grad = jnp.sum(two_delta * hidden_two.astype(f32), axis=0) / feed_gain
    two_local = scatter_tokens(two_delta, bf16, *where)
    mid_delta = cotangent + norm_back(two_local * feed_gain, mid * scale_two, scale_two)
    mid_low = gather_tokens(mid_delta.astype(bf16), *where)
    branch_delta = mm(mid_low, attn[:, 896:], NN)
    gate_low, head_gain_grad, mixed_delta, pack = call(
        head_back_body,
        [(tall, bf16), ((1, VDIM), f32), (tall, f32), ((VDIM + STATE_PAD, KDIM), bf16)],
        branch_delta, unit, scale_head, proj, head_gain, opened, through,
    )
    query_d, key_d, value_d = call(
        within_back_body,
        [(wide, f32), (wide, f32), (tall, f32)],
        mixed_delta, proj, sums, scores, seg_col, seg_row, seg_before, state_in,
    )
    out_grad = mm(mid_low, branch, TN).astype(bf16)
    state_grad = scan_states(pack, True)
    low_one, up_grad, bias_grad = call(
        state_back_body,
        [((count, 896), bf16), ((RANK, KDIM), f32), ((1, KDIM), f32)],
        query_d, key_d, value_d, state_grad, state_in, state_end, through, proj, sums, kept,
        logits, seg_col, up3, gate_low,
    )
    one_delta = mm(low_one, attn[:, :896], NT)
    main_grad = mm(hidden_one, low_one, TN)
    mixer_gain_grad = jnp.sum(one_delta * hidden_one.astype(f32), axis=0) / mixer_gain
    depth = main_grad.shape[0]
    tensor_index, section_index = where
    head = tensor_index * 2 + section_index
    ranks = jnp.concatenate([up_grad.T, bias_grad.T, jnp.zeros((KDIM, 1), f32)], axis=1)
    ranks = lax.dynamic_update_slice(
        jnp.zeros((HEADS * KDIM, RANK + 2), f32), ranks, (head * KDIM, 0)
    ).reshape(depth, -1)
    repeat = depth // VDIM
    gains = jnp.broadcast_to(head_gain_grad.reshape(VDIM, 1), (VDIM, repeat)).reshape(depth, 1)
    smalls = jnp.concatenate(
        [main_grad[:, 768:784], mixer_gain_grad[:, None], feed_gain_grad[:, None], ranks, gains],
        axis=1,
    )
    smalls = jnp.pad(smalls, ((0, 0), (0, PACK - smalls.shape[1])))
    attn_grad = jnp.concatenate(
        [main_grad[:, :768].astype(bf16), smalls.astype(bf16), out_grad], axis=1
    )
    attn_reduced = lax.psum_scatter(attn_grad, "dp", scatter_dimension=0, tiled=True)
    one_local = scatter_tokens(one_delta, bf16, *where)
    input_delta = mid_delta + norm_back(one_local * mixer_gain, layer_in * scale_one, scale_one)
    return input_delta, attn_reduced, feed_reduced


def in_three(values):
    high = lax.reduce_precision(values, 8, 7)
    rest = values - high
    middle = lax.reduce_precision(rest, 8, 7)
    return [high.astype(bf16), middle.astype(bf16), (rest - middle).astype(bf16)]


def small_params(attn, tensor_index, section_index):
    depth = attn.shape[0]
    pack = attn[:, 768:896].astype(f32)
    rest = pack[:, 48:60] + pack[:, 60:72] + pack[:, 72:84]
    ranks = rest[:, 2:11].reshape(HEADS * KDIM, RANK + 2)
    head = tensor_index * 2 + section_index
    ranks = lax.dynamic_slice_in_dim(ranks, head * KDIM, KDIM, 0).T
    up = ranks[:RANK]
    up3 = jnp.concatenate([up, up, up, jnp.zeros((PACK - 3 * RANK, KDIM), f32)], axis=0)
    head_gain = rest[:, 11].reshape(VDIM, depth // VDIM)[:, 0]
    return rest[:, 0], rest[:, 1], up3, ranks[RANK : RANK + 1], head_gain[None]


def shards(
    inputs, segments, mixer_gain, query_weight, key_weight, value_weight, outgate_weight,
    decay_down, decay_up, decay_bias, head_gain, output_weight, feed_gain, gate_weight,
    up_weight, down_weight, cotangent,
):
    section_index = lax.axis_index("section")
    tensor_index = lax.axis_index("tensor")
    dp_index = lax.axis_index("dp")
    where = (tensor_index, section_index)
    left, first = section_index == 0, tensor_index == 0
    segment_ids = segments.astype(f32)
    count = segment_ids.shape[0]

    narrow = mixer_gain.shape[1]
    ranks = jnp.concatenate(
        [decay_up[0].T, decay_bias[0][:, None], jnp.zeros((decay_bias.shape[1], 1), f32)], axis=1
    ).reshape(narrow, -1)
    spread = narrow // head_gain.shape[1]
    gains = jnp.broadcast_to(head_gain[0][:, None], (head_gain.shape[1], spread)).reshape(narrow, 1)
    mine = jnp.concatenate(
        [decay_down[0], mixer_gain[0][:, None], feed_gain[0][:, None], ranks, gains], axis=1
    )
    theirs = swap(mine, "tensor")
    rows = jnp.concatenate([jnp.where(first, mine, theirs), jnp.where(first, theirs, mine)], axis=0)
    seg_end = jnp.broadcast_to(segment_ids[-1:][None], (2 * narrow, 1)).astype(bf16)
    pack = jnp.concatenate(in_three(rows[:, :RANK]) + in_three(rows[:, RANK:]) + [seg_end], axis=1)
    pack = jnp.pad(pack, ((0, 0), (0, PACK - pack.shape[1])))

    def half(weight, side):
        width = weight.shape[1] // 2
        return weight[:, side * width : (side + 1) * width]

    out_t, down_t = output_weight[0].T, down_weight[0].T

    def attn_half(side):
        parts = [half(w, side) for w in (query_weight[0], key_weight[0], value_weight[0], outgate_weight[0])]
        return jnp.concatenate(parts + [pack, half(out_t, side)], axis=1)

    def feed_half(side):
        parts = [half(w, side) for w in (gate_weight[0], up_weight[0], down_t)]
        return jnp.concatenate(parts, axis=1)

    def per_layer(side_zero, side_one):
        keep = jnp.where(left, side_zero, side_one)
        got = swap(jnp.where(left, side_one, side_zero), "section")
        return jnp.where(left, keep, got), jnp.where(left, got, keep)

    attn_parts = per_layer(attn_half(0), attn_half(1))
    feed_parts = per_layer(feed_half(0), feed_half(1))
    attn, feed = [], []
    for layer in range(2):
        attn.append(lax.all_gather(attn_parts[layer], "dp", axis=0, tiled=True))
        feed.append(lax.all_gather(feed_parts[layer], "dp", axis=0, tiled=True))
    params = [(attn[k], feed[k], small_params(attn[k], *where)) for k in range(2)]
    wide = 2 * narrow
    earlier = lax.dynamic_slice(
        attn[0], (jnp.maximum(dp_index - 1, 0) * wide, 768 + 84), (1, 1)
    ).astype(f32)
    seg_before = jnp.where(dp_index == 0, -1.0, earlier)
    seg = (segment_ids[:, None], segment_ids[None, :], seg_before)

    own = inputs.shape[0] // 2
    layer_in = lax.dynamic_slice_in_dim(inputs, section_index * own, own, 0)
    cot = lax.dynamic_slice_in_dim(cotangent, section_index * own, own, 0)
    out0, saved0 = layer_forward(layer_in, seg, params[0], where)
    out1, saved1 = layer_forward(out0, seg, params[1], where)
    delta1, attn_red1, feed_red1 = layer_backward(saved1, cot, seg, params[1], where)
    delta0, attn_red0, feed_red0 = layer_backward(saved0, delta1, seg, params[0], where)

    def to_section(of_zero, of_one):
        keep = jnp.where(left, of_zero, of_one)
        got = swap(jnp.where(left, of_one, of_zero), "section")
        return keep, got

    def joined(keep, got, axis):
        return jnp.concatenate([jnp.where(left, keep, got), jnp.where(left, got, keep)], axis=axis)

    section_out = joined(*to_section(out0, out1), 0)
    input_grad = joined(*to_section(delta0, delta1), 0)
    attn_keep, attn_got = to_section(attn_red0, attn_red1)
    feed_keep, feed_got = to_section(feed_red0, feed_red1)

    def columns(keep, got, start, width):
        return joined(keep[:, start : start + width], got[:, start : start + width], 1).astype(f32)

    units = feed_keep.shape[1] // 3
    small = attn_keep[:, 768:896].astype(f32) + attn_got[:, 768:896].astype(f32)
    small_mine = jnp.where(first, small[:narrow], small[narrow:])
    small_theirs = jnp.where(first, small[narrow:], small[:narrow])
    small = small_mine + swap(small_theirs, "tensor")
    ranks = small[:, 18:27].reshape(decay_bias.shape[1], RANK + 2)
    outs = (
        section_out,
        input_grad,
        small[:, 16],
        columns(attn_keep, attn_got, 0, 128),
        columns(attn_keep, attn_got, 128, 128),
        columns(attn_keep, attn_got, 256, 256),
        columns(attn_keep, attn_got, 512, 256),
        small[:, :16],
        ranks[:, :RANK].T,
        ranks[:, RANK],
        small[:, 27].reshape(-1, spread)[:, 0],
        columns(attn_keep, attn_got, 896, 256).T,
        small[:, 17],
        columns(feed_keep, feed_got, 0, units),
        columns(feed_keep, feed_got, units, units),
        columns(feed_keep, feed_got, 2 * units, units).T,
    )
    return tuple(out[None] for out in outs)


def solution(mesh):
    rows = P(("dp", "tensor"), None)
    vector = P("section", ("dp", "tensor"))
    down_in = P("section", "dp", "tensor")
    up_out = P("section", "tensor", "dp")
    placed = (
        rows, P("dp"), vector, down_in, down_in, down_in, down_in,
        P("section", ("dp", "tensor"), None), P("section", None, ("dp", "tensor")),
        vector, vector, up_out, vector, down_in, down_in, up_out, rows,
    )
    tokens = P("section", ("dp", "tensor"), None)
    return jax.shard_map(
        shards,
        mesh=mesh,
        in_specs=placed,
        out_specs=(
            tokens, tokens, vector, down_in, down_in, down_in, down_in, tokens,
            P("section", None, ("dp", "tensor")), vector, vector, up_out, vector,
            down_in, down_in, up_out,
        ),
        check_vma=False,
    )
```

```python
import functools

import jax
import jax.numpy as jnp
from jax import lax
from jax.experimental import pallas as pl
from jax.experimental.pallas import tpu as pltpu
from jax.sharding import PartitionSpec as P

HEADS = 4
KDIM = 128
VDIM = 256
RANK = 16
SUB = 16
PACK = 128
STATE_PAD = 16

norm_eps = 1e-06
head_eps = 1e-05
f32 = jnp.float32
bf16 = jnp.bfloat16
INTERPRET = False


def swap(block, axis):
    return lax.ppermute(block, axis, [(0, 1), (1, 0)])


def mm(left, right, dims):
    return lax.dot_general(left, right, (dims, ((), ())), preferred_element_type=f32)


def exact(left, right, dims=((1,), (0,))):
    return lax.dot_general(
        left, right, (dims, ((), ())), precision=lax.Precision.HIGHEST, preferred_element_type=f32
    )


NN = ((1,), (0,))
NT = ((1,), (1,))
TN = ((0,), (0,))


def call(body, outs, *args):
    return pl.pallas_call(
        body,
        out_shape=[jax.ShapeDtypeStruct(shape, kind) for shape, kind in outs],
        interpret=INTERPRET,
    )(*args)


def iota2(rows, cols, axis):
    return lax.broadcasted_iota(jnp.int32, (rows, cols), axis)


def lower(count):
    return jnp.where(iota2(count, count, 0) >= iota2(count, count, 1), 1.0, 0.0)


def levels(count):
    half, out = count // 2, []
    while half >= SUB:
        out.append(half)
        half //= 2
    return out


def level_factors(sums, half):
    count, width = sums.shape
    parts = sums.reshape(count // (2 * half), 2 * half, width)
    middle = jnp.broadcast_to(parts[:, half - 1 : half, :], parts.shape).reshape(count, width)
    late = (iota2(count, width, 0) & half) != 0
    gap = sums - middle
    to_late = jnp.where(late, jnp.exp(jnp.minimum(gap, 0.0)), 0.0)
    to_early = jnp.where(late, 0.0, jnp.exp(jnp.minimum(-gap, 0.0)))
    return to_late, to_early


def level_mask(count, half):
    rows, cols = iota2(count, count, 0), iota2(count, count, 1)
    bits = 2 * half - 1
    return (rows & ~bits) == (cols & ~bits)


def pair_mask(seg_col, seg_row, count):
    same = seg_col == seg_row
    return same & (iota2(count, count, 0) >= iota2(count, count, 1))


def pick_mask(count, offset):
    rows, cols = iota2(count, count, 0), iota2(count, count, 1)
    return cols == ((rows & ~(SUB - 1)) + offset)


def sub_factor(sums3, offset):
    return jnp.exp(jnp.minimum(sums3 - sums3[:, offset : offset + 1, :], 0.0))


def pre_body(
    proj, up3, bias, seg_col, seg_before, logits_o, sums_o, open_o, keep_o, end_o, through_o, pack_o
):
    count = proj.shape[0]
    logits = exact(proj[:, 768:896], up3[...]) + bias[...]
    decay = (jnp.minimum(logits, 0.0) - jnp.log1p(jnp.exp(-jnp.abs(logits)))) / 16.0
    sums = exact(lower(count), decay)
    last = sums[count - 1 : count, :]
    seg = seg_col[...]
    seg_last = seg[count - 1 : count, :]
    before = seg_before[...]
    opened = jnp.where(seg == before, proj[:, 0:128] * jnp.exp(sums), 0.0)
    kept = jnp.where(seg == seg_last, proj[:, 128:256] * jnp.exp(last - sums), 0.0)
    state = exact(proj[:, 256:512], kept, TN)
    through = jnp.where(before == seg_last, jnp.exp(last), 0.0)
    logits_o[...] = logits
    sums_o[...] = sums
    open_o[...] = opened
    keep_o[...] = kept
    end_o[...] = state
    through_o[...] = through
    pack_o[0:VDIM, :] = state.astype(bf16)
    pack_o[VDIM : VDIM + STATE_PAD, :] = jnp.broadcast_to(through, (STATE_PAD, KDIM)).astype(bf16)


def within_body(proj, sums_r, seg_col, seg_row, scores_o, out_o):
    count = proj.shape[0]
    query, key = proj[:, 0:128], proj[:, 128:256]
    sums = sums_r[...]
    scores = jnp.zeros((count, count), f32)
    for half in levels(count):
        to_late, to_early = level_factors(sums, half)
        part = exact(query * to_late, key * to_early, NT)
        scores = scores + jnp.where(level_mask(count, half), part, 0.0)
    blocks = (count // SUB, SUB, KDIM)
    query3, key3, sums3 = query.reshape(blocks), key.reshape(blocks), sums.reshape(blocks)
    for offset in range(SUB):
        weight = sub_factor(sums3, offset)
        column = jnp.sum(query3 * weight * key3[:, offset : offset + 1, :], axis=-1, keepdims=True)
        scores = jnp.where(pick_mask(count, offset), column.reshape(count, 1), scores)
    scores = jnp.where(pair_mask(seg_col[...], seg_row[...], count), scores, 0.0)
    scores_o[...] = scores
    out_o[...] = exact(scores, proj[:, 256:512])


def post_body(within, opened, state_in, proj, gain, unit_o, scale_o, branch_o):
    mixed = within[...] + exact(opened[...], state_in[...], NT)
    scale = lax.rsqrt(jnp.mean(mixed * mixed, axis=-1, keepdims=True) + head_eps)
    unit = mixed * scale
    gate = proj[:, 512:768]
    unit_o[...] = unit
    scale_o[...] = scale
    branch_o[...] = (unit * gain[...] * (gate * jax.nn.sigmoid(gate))).astype(bf16)


def head_back_body(
    branch_delta, unit_r, scale, proj, gain_r, opened, through, low_o, gain_o, mixed_o, pack_o
):
    delta, unit, gate, gain = branch_delta[...], unit_r[...], proj[:, 512:768], gain_r[...]
    sigma = jax.nn.sigmoid(gate)
    swish = gate * sigma
    slope = sigma * (1.0 + gate * (1.0 - sigma))
    low_o[...] = (delta * unit * gain * slope).astype(bf16)
    through_unit = delta * swish
    gain_o[...] = jnp.sum(through_unit * unit, axis=0, keepdims=True)
    inner = through_unit * gain
    mixed = scale[...] * (inner - unit * jnp.mean(inner * unit, axis=-1, keepdims=True))
    mixed_o[...] = mixed
    pack_o[0:VDIM, :] = exact(mixed, opened[...], TN).astype(bf16)
    pack_o[VDIM : VDIM + STATE_PAD, :] = jnp.broadcast_to(
        through[...], (STATE_PAD, KDIM)
    ).astype(bf16)


def within_back_body(
    mixed_r, proj, sums_r, scores, seg_col, seg_row, seg_before, state_in, query_o, key_o, value_o
):
    count = proj.shape[0]
    query, key, value = proj[:, 0:128], proj[:, 128:256], proj[:, 256:512]
    sums, mixed = sums_r[...], mixed_r[...]
    value_o[...] = exact(scores[...], mixed, TN)
    grad = jnp.where(
        pair_mask(seg_col[...], seg_row[...], count), exact(mixed, value, NT), 0.0
    )
    query_delta = jnp.where(
        seg_col[...] == seg_before[...], jnp.exp(sums) * exact(mixed, state_in[...]), 0.0
    )
    key_delta = jnp.zeros((count, KDIM), f32)
    for half in levels(count):
        to_late, to_early = level_factors(sums, half)
        part = jnp.where(level_mask(count, half), grad, 0.0)
        query_delta = query_delta + to_late * exact(part, key * to_early)
        key_delta = key_delta + to_early * exact(part, query * to_late, TN)
    blocks = (count // SUB, SUB, KDIM)
    query3, key3, sums3 = query.reshape(blocks), key.reshape(blocks), sums.reshape(blocks)
    place = lax.broadcasted_iota(jnp.int32, blocks, 1)
    query_sub, key_sub = jnp.zeros(blocks, f32), jnp.zeros(blocks, f32)
    for offset in range(SUB):
        weight = sub_factor(sums3, offset)
        column = jnp.sum(jnp.where(pick_mask(count, offset), grad, 0.0), axis=-1, keepdims=True)
        weighted = weight * column.reshape(count // SUB, SUB, 1)
        query_sub = query_sub + weighted * key3[:, offset : offset + 1, :]
        total = jnp.sum(weighted * query3, axis=1, keepdims=True)
        key_sub = jnp.where(place == offset, total, key_sub)
    query_o[...] = query_delta + query_sub.reshape(count, KDIM)
    key_o[...] = key_delta + key_sub.reshape(count, KDIM)


def state_back_body(
    query_d, key_d, value_d, state_grad, state_in, state_end, through, proj, sums_r, kept,
    logits, seg_col, up3, gate_low, low_o, up_o, bias_o,
):
    count = proj.shape[0]
    grad, sums = state_grad[...], sums_r[...]
    last = sums[count - 1 : count, :]
    seg = seg_col[...]
    query_delta = query_d[...]
    value_delta = value_d[...] + exact(kept[...], grad, NT)
    key_delta = key_d[...] + jnp.where(
        seg == seg[count - 1 : count, :],
        jnp.exp(last - sums) * exact(proj[:, 256:512], grad),
        0.0,
    )
    final = state_end[...] + through[...] * state_in[...]
    beyond = jnp.sum(final * grad, axis=0, keepdims=True)
    local = proj[:, 0:128] * query_delta - proj[:, 128:256] * key_delta
    decay_delta = exact(lower(count), local, TN) + beyond
    logit_delta = decay_delta * jax.nn.sigmoid(-logits[...]) / 16.0
    bias_o[...] = jnp.sum(logit_delta, axis=0, keepdims=True)
    ranks = exact(proj[:, 768:896], logit_delta, TN)
    up_o[...] = ranks[0:16, :] + ranks[16:32, :] + ranks[32:48, :]
    low_o[:, 0:128] = query_delta.astype(bf16)
    low_o[:, 128:256] = key_delta.astype(bf16)
    low_o[:, 256:512] = value_delta.astype(bf16)
    low_o[:, 512:768] = gate_low[...]
    low_o[:, 768:896] = exact(logit_delta, up3[...], NT).astype(bf16)


def scan_states(pack, backward):
    count = lax.axis_size("dp")
    here = lax.axis_index("dp")
    state = pack[:VDIM].astype(f32)
    through = pack[VDIM : VDIM + 1].astype(f32)
    carried, passed = jnp.zeros_like(state), jnp.ones_like(through)
    step = 1
    while step < count:
        other = lax.ppermute(pack, "dp", [(i, i ^ step) for i in range(count)])
        other_state = other[:VDIM].astype(f32)
        other_through = other[VDIM : VDIM + 1].astype(f32)
        mine_later = (here & step) != 0
        ahead = jnp.logical_not(mine_later) if backward else mine_later
        carried = jnp.where(ahead, carried + passed * other_state, carried)
        passed = jnp.where(ahead, passed * other_through, passed)
        state = jnp.where(ahead, state + through * other_state, other_state + other_through * state)
        through = through * other_through
        step *= 2
        if step < count:
            pack = jnp.concatenate(
                [state, jnp.broadcast_to(through, (STATE_PAD, KDIM))], axis=0
            ).astype(bf16)
    return carried


def gather_tokens(block, tensor_index, section_index):
    other = swap(block, "tensor")
    first = tensor_index == 0
    pair = jnp.stack([jnp.where(first, block, other), jnp.where(first, other, block)])
    far = swap(pair, "section")
    left = section_index == 0
    whole = jnp.stack([jnp.where(left, pair, far), jnp.where(left, far, pair)], axis=1)
    return whole.reshape(4 * block.shape[0], block.shape[1])


def scatter_tokens(partial, kind, tensor_index, section_index):
    rows = partial.shape[0] // 4
    parts = partial.reshape(2, 2, rows, partial.shape[1])
    left = section_index == 0
    keep = jnp.where(left, parts[:, 0], parts[:, 1])
    send = jnp.where(left, parts[:, 1], parts[:, 0])
    both = keep + swap(send, "section")
    first = tensor_index == 0
    mine = jnp.where(first, both[0], both[1])
    theirs = jnp.where(first, both[1], both[0]).astype(kind)
    return mine + swap(theirs, "tensor").astype(f32)


def rms_scale(values, epsilon):
    return lax.rsqrt(jnp.mean(values * values, axis=-1, keepdims=True) + epsilon)


def norm_back(grad_unit, unit_values, scale_values):
    return scale_values * (
        grad_unit - unit_values * jnp.mean(grad_unit * unit_values, axis=-1, keepdims=True)
    )


def layer_forward(layer_in, seg, params, where):
    attn, feed, small = params
    mixer_gain, feed_gain, up3, bias, head_gain = small
    seg_col, seg_row, seg_before = seg
    count = seg_col.shape[0]
    scale_one = rms_scale(layer_in, norm_eps)
    hidden_one = gather_tokens((layer_in * scale_one * mixer_gain).astype(bf16), *where)
    proj = mm(hidden_one, attn[:, :896], NN)
    wide, tall = (count, KDIM), (count, VDIM)
    logits, sums, opened, kept, state_end, through, pack = call(
        pre_body,
        [(wide, f32)] * 4
        + [((VDIM, KDIM), f32), ((1, KDIM), f32), ((VDIM + STATE_PAD, KDIM), bf16)],
        proj, up3, bias, seg_col, seg_before,
    )
    scores, within = call(
        within_body, [((count, count), f32), (tall, f32)], proj, sums, seg_col, seg_row
    )
    state_in = scan_states(pack, False)
    unit, scale_head, branch = call(
        post_body,
        [(tall, f32), ((count, 1), f32), (tall, bf16)],
        within, opened, state_in, proj, head_gain,
    )
    mid = layer_in + scatter_tokens(mm(branch, attn[:, 896:], NT), f32, *where)
    scale_two = rms_scale(mid, norm_eps)
    hidden_two = gather_tokens((mid * scale_two * feed_gain).astype(bf16), *where)
    units = feed.shape[1] // 3
    both = mm(hidden_two, feed[:, : 2 * units], NN)
    gate_pre, up_pre = both[:, :units], both[:, units:]
    inner = (jax.nn.silu(gate_pre) * up_pre).astype(bf16)
    result = mid + scatter_tokens(mm(inner, feed[:, 2 * units :], NT), f32, *where)
    saved = (
        layer_in, scale_one, hidden_one, proj, logits, sums, opened, kept, state_end, through,
        scores, state_in, unit, scale_head, branch, mid, scale_two, hidden_two, both, inner,
    )
    return result, saved


def scattered(grad):
    return lax.psum_scatter(grad, "dp", scatter_dimension=0, tiled=True)


def layer_backward(saved, cotangent, seg, params, where, pending, earlier):
    attn, feed, small = params
    mixer_gain, feed_gain, up3, bias, head_gain = small
    seg_col, seg_row, seg_before = seg
    (
        layer_in, scale_one, hidden_one, proj, logits, sums, opened, kept, state_end, through,
        scores, state_in, unit, scale_head, branch, mid, scale_two, hidden_two, both, inner,
    ) = saved
    count = seg_col.shape[0]
    wide, tall = (count, KDIM), (count, VDIM)
    units = feed.shape[1] // 3
    cot = gather_tokens(cotangent.astype(bf16), *where)
    inner_delta = mm(cot, feed[:, 2 * units :], NN)
    gate_pre, up_pre = both[:, :units], both[:, units:]
    sigma = jax.nn.sigmoid(gate_pre)
    gate_delta = inner_delta * up_pre * (sigma * (1.0 + gate_pre * (1.0 - sigma)))
    up_delta = inner_delta * (gate_pre * sigma)
    low_two = jnp.concatenate([gate_delta, up_delta], axis=1).astype(bf16)
    two_delta = mm(low_two, feed[:, : 2 * units], NT)
    feed_grad = jnp.concatenate(
        pending + [mm(hidden_two, low_two, TN).astype(bf16), mm(cot, inner, TN).astype(bf16)],
        axis=1,
    )
    feed_gain_grad = jnp.sum(two_delta * hidden_two.astype(f32), axis=0) / feed_gain
    two_local = scatter_tokens(two_delta, bf16, *where)
    mid_delta = cotangent + norm_back(two_local * feed_gain, mid * scale_two, scale_two)
    mid_delta, feed_grad = lax.optimization_barrier((mid_delta, feed_grad))
    feed_reduced = scattered(feed_grad)
    mid_low = gather_tokens(mid_delta.astype(bf16), *where)
    branch_delta = mm(mid_low, attn[:, 896:], NN)
    gate_low, head_gain_grad, mixed_delta, pack = call(
        head_back_body,
        [(tall, bf16), ((1, VDIM), f32), (tall, f32), ((VDIM + STATE_PAD, KDIM), bf16)],
        branch_delta, unit, scale_head, proj, head_gain, opened, through,
    )
    query_d, key_d, value_d = call(
        within_back_body,
        [(wide, f32), (wide, f32), (tall, f32)],
        mixed_delta, proj, sums, scores, seg_col, seg_row, seg_before, state_in,
    )
    out_grad = mm(mid_low, branch, TN).astype(bf16)
    state_grad = scan_states(pack, True)
    low_one, up_grad, bias_grad = call(
        state_back_body,
        [((count, 896), bf16), ((RANK, KDIM), f32), ((1, KDIM), f32)],
        query_d, key_d, value_d, state_grad, state_in, state_end, through, proj, sums, kept,
        logits, seg_col, up3, gate_low,
    )
    low_one, earlier = lax.optimization_barrier((low_one, earlier))
    one_delta = mm(low_one, attn[:, :896], NT)
    main_grad = mm(hidden_one, low_one, TN)
    mixer_gain_grad = jnp.sum(one_delta * hidden_one.astype(f32), axis=0) / mixer_gain
    depth = main_grad.shape[0]
    tensor_index, section_index = where
    head = tensor_index * 2 + section_index
    ranks = jnp.concatenate([up_grad.T, bias_grad.T, jnp.zeros((KDIM, 1), f32)], axis=1)
    ranks = lax.dynamic_update_slice(
        jnp.zeros((HEADS * KDIM, RANK + 2), f32), ranks, (head * KDIM, 0)
    ).reshape(depth, -1)
    repeat = depth // VDIM
    gains = jnp.broadcast_to(head_gain_grad.reshape(VDIM, 1), (VDIM, repeat)).reshape(depth, 1)
    smalls = jnp.concatenate(
        [main_grad[:, 768:784], mixer_gain_grad[:, None], feed_gain_grad[:, None], ranks, gains],
        axis=1,
    )
    smalls = jnp.pad(smalls, ((0, 0), (0, PACK - smalls.shape[1])))
    attn_grad = jnp.concatenate(
        [main_grad[:, :768].astype(bf16), smalls.astype(bf16), out_grad], axis=1
    )
    one_local = scatter_tokens(one_delta, bf16, *where)
    input_delta = mid_delta + norm_back(one_local * mixer_gain, layer_in * scale_one, scale_one)
    input_delta, attn_grad = lax.optimization_barrier((input_delta, attn_grad))
    return input_delta, attn_grad, feed_reduced, earlier


def in_three(values):
    high = lax.reduce_precision(values, 8, 7)
    rest = values - high
    middle = lax.reduce_precision(rest, 8, 7)
    return [high.astype(bf16), middle.astype(bf16), (rest - middle).astype(bf16)]


def small_params(attn, tensor_index, section_index):
    depth = attn.shape[0]
    pack = attn[:, 768:896].astype(f32)
    rest = pack[:, 48:60] + pack[:, 60:72] + pack[:, 72:84]
    ranks = rest[:, 2:11].reshape(HEADS * KDIM, RANK + 2)
    head = tensor_index * 2 + section_index
    ranks = lax.dynamic_slice_in_dim(ranks, head * KDIM, KDIM, 0).T
    up = ranks[:RANK]
    up3 = jnp.concatenate([up, up, up, jnp.zeros((PACK - 3 * RANK, KDIM), f32)], axis=0)
    head_gain = rest[:, 11].reshape(VDIM, depth // VDIM)[:, 0]
    return rest[:, 0], rest[:, 1], up3, ranks[RANK : RANK + 1], head_gain[None]


def shards(
    inputs, segments, mixer_gain, query_weight, key_weight, value_weight, outgate_weight,
    decay_down, decay_up, decay_bias, head_gain, output_weight, feed_gain, gate_weight,
    up_weight, down_weight, cotangent,
):
    section_index = lax.axis_index("section")
    tensor_index = lax.axis_index("tensor")
    dp_index = lax.axis_index("dp")
    where = (tensor_index, section_index)
    left, first = section_index == 0, tensor_index == 0
    segment_ids = segments.astype(f32)
    count = segment_ids.shape[0]

    narrow = mixer_gain.shape[1]
    ranks = jnp.concatenate(
        [decay_up[0].T, decay_bias[0][:, None], jnp.zeros((decay_bias.shape[1], 1), f32)], axis=1
    ).reshape(narrow, -1)
    spread = narrow // head_gain.shape[1]
    gains = jnp.broadcast_to(head_gain[0][:, None], (head_gain.shape[1], spread)).reshape(narrow, 1)
    mine = jnp.concatenate(
        [decay_down[0], mixer_gain[0][:, None], feed_gain[0][:, None], ranks, gains], axis=1
    )
    theirs = swap(mine, "tensor")
    rows = jnp.concatenate([jnp.where(first, mine, theirs), jnp.where(first, theirs, mine)], axis=0)
    seg_end = jnp.broadcast_to(segment_ids[-1:][None], (2 * narrow, 1)).astype(bf16)
    pack = jnp.concatenate(in_three(rows[:, :RANK]) + in_three(rows[:, RANK:]) + [seg_end], axis=1)
    pack = jnp.pad(pack, ((0, 0), (0, PACK - pack.shape[1])))

    def half(weight, side):
        width = weight.shape[1] // 2
        return weight[:, side * width : (side + 1) * width]

    out_t, down_t = output_weight[0].T, down_weight[0].T

    def attn_half(side):
        parts = [half(w, side) for w in (query_weight[0], key_weight[0], value_weight[0], outgate_weight[0])]
        return jnp.concatenate(parts + [pack, half(out_t, side)], axis=1)

    def feed_half(side):
        parts = [half(w, side) for w in (gate_weight[0], up_weight[0], down_t)]
        return jnp.concatenate(parts, axis=1)

    def per_layer(side_zero, side_one):
        keep = jnp.where(left, side_zero, side_one)
        got = swap(jnp.where(left, side_one, side_zero), "section")
        return jnp.where(left, keep, got), jnp.where(left, got, keep)

    attn_parts = per_layer(attn_half(0), attn_half(1))
    feed_parts = per_layer(feed_half(0), feed_half(1))

    def gathered(part):
        return lax.all_gather(part, "dp", axis=0, tiled=True)

    attn_width = attn_parts[0].shape[1]
    attn0 = gathered(attn_parts[0])
    middle = gathered(jnp.concatenate([attn_parts[1], feed_parts[0]], axis=1))
    feed1 = gathered(feed_parts[1])
    wide = 2 * narrow
    earlier = lax.dynamic_slice(
        attn0, (jnp.maximum(dp_index - 1, 0) * wide, 768 + 84), (1, 1)
    ).astype(f32)
    seg_before = jnp.where(dp_index == 0, -1.0, earlier)
    seg = (segment_ids[:, None], segment_ids[None, :], seg_before)

    own = inputs.shape[0] // 2
    layer_in = lax.dynamic_slice_in_dim(inputs, section_index * own, own, 0)
    cot = lax.dynamic_slice_in_dim(cotangent, section_index * own, own, 0)
    params0 = (attn0, middle[:, attn_width:], small_params(attn0, *where))
    out0, saved0 = layer_forward(layer_in, seg, params0, where)
    late, out0 = lax.optimization_barrier((middle, out0))
    attn1 = late[:, :attn_width]
    params1 = (attn1, feed1, small_params(attn1, *where))
    out1, saved1 = layer_forward(out0, seg, params1, where)
    delta1, attn_grad1, feed_red1, _ = layer_backward(saved1, cot, seg, params1, where, [], [])
    delta0, attn_grad0, mixed_red, (feed_red1,) = layer_backward(
        saved0, delta1, seg, params0, where, [attn_grad1], [feed_red1]
    )
    attn_grad0, mixed_red = lax.optimization_barrier((attn_grad0, mixed_red))
    attn_red1, feed_red0 = mixed_red[:, :attn_width], mixed_red[:, attn_width:]
    attn_red0 = scattered(attn_grad0)

    def to_section(of_zero, of_one):
        keep = jnp.where(left, of_zero, of_one)
        got = swap(jnp.where(left, of_one, of_zero), "section")
        return keep, got

    def joined(keep, got, axis):
        return jnp.concatenate([jnp.where(left, keep, got), jnp.where(left, got, keep)], axis=axis)

    section_out = joined(*to_section(out0, out1), 0)
    input_grad = joined(*to_section(delta0, delta1), 0)
    attn_keep, attn_got = to_section(attn_red0, attn_red1)
    feed_keep, feed_got = to_section(feed_red0, feed_red1)

    def columns(keep, got, start, width):
        return joined(keep[:, start : start + width], got[:, start : start + width], 1).astype(f32)

    units = feed_keep.shape[1] // 3
    small = attn_keep[:, 768:896].astype(f32) + attn_got[:, 768:896].astype(f32)
    small_mine = jnp.where(first, small[:narrow], small[narrow:])
    small_theirs = jnp.where(first, small[narrow:], small[:narrow])
    small = small_mine + swap(small_theirs, "tensor")
    ranks = small[:, 18:27].reshape(decay_bias.shape[1], RANK + 2)
    outs = (
        section_out,
        input_grad,
        small[:, 16],
        columns(attn_keep, attn_got, 0, 128),
        columns(attn_keep, attn_got, 128, 128),
        columns(attn_keep, attn_got, 256, 256),
        columns(attn_keep, attn_got, 512, 256),
        small[:, :16],
        ranks[:, :RANK].T,
        ranks[:, RANK],
        small[:, 27].reshape(-1, spread)[:, 0],
        columns(attn_keep, attn_got, 896, 256).T,
        small[:, 17],
        columns(feed_keep, feed_got, 0, units),
        columns(feed_keep, feed_got, units, units),
        columns(feed_keep, feed_got, 2 * units, units).T,
    )
    return tuple(out[None] for out in outs)


def solution(mesh):
    rows = P(("dp", "tensor"), None)
    vector = P("section", ("dp", "tensor"))
    down_in = P("section", "dp", "tensor")
    up_out = P("section", "tensor", "dp")
    placed = (
        rows, P("dp"), vector, down_in, down_in, down_in, down_in,
        P("section", ("dp", "tensor"), None), P("section", None, ("dp", "tensor")),
        vector, vector, up_out, vector, down_in, down_in, up_out, rows,
    )
    tokens = P("section", ("dp", "tensor"), None)
    return jax.shard_map(
        shards,
        mesh=mesh,
        in_specs=placed,
        out_specs=(
            tokens, tokens, vector, down_in, down_in, down_in, down_in, tokens,
            P("section", None, ("dp", "tensor")), vector, vector, up_out, vector,
            down_in, down_in, up_out,
        ),
        check_vma=False,
    )
```

```python
import functools

import jax
import jax.numpy as jnp
from jax import lax
from jax.experimental import pallas as pl
from jax.experimental.pallas import tpu as pltpu
from jax.sharding import PartitionSpec as P

HEADS = 4
KDIM = 128
VDIM = 256
RANK = 16
SUB = 16
PACK = 128
STATE_PAD = 16

norm_eps = 1e-06
head_eps = 1e-05
f32 = jnp.float32
bf16 = jnp.bfloat16
INTERPRET = False


def swap(block, axis):
    return lax.ppermute(block, axis, [(0, 1), (1, 0)])


def mm(left, right, dims):
    return lax.dot_general(left, right, (dims, ((), ())), preferred_element_type=f32)


def exact(left, right, dims=((1,), (0,))):
    return lax.dot_general(
        left, right, (dims, ((), ())), precision=lax.Precision.HIGHEST, preferred_element_type=f32
    )


NN = ((1,), (0,))
NT = ((1,), (1,))
TN = ((0,), (0,))


def call(body, outs, *args):
    return pl.pallas_call(
        body,
        out_shape=[jax.ShapeDtypeStruct(shape, kind) for shape, kind in outs],
        interpret=INTERPRET,
    )(*args)


def iota2(rows, cols, axis):
    return lax.broadcasted_iota(jnp.int32, (rows, cols), axis)


def lower(count):
    return jnp.where(iota2(count, count, 0) >= iota2(count, count, 1), 1.0, 0.0)


def levels(count):
    half, out = count // 2, []
    while half >= SUB:
        out.append(half)
        half //= 2
    return out


def level_factors(sums, half):
    count, width = sums.shape
    parts = sums.reshape(count // (2 * half), 2 * half, width)
    middle = jnp.broadcast_to(parts[:, half - 1 : half, :], parts.shape).reshape(count, width)
    late = (iota2(count, width, 0) & half) != 0
    gap = sums - middle
    to_late = jnp.where(late, jnp.exp(jnp.minimum(gap, 0.0)), 0.0)
    to_early = jnp.where(late, 0.0, jnp.exp(jnp.minimum(-gap, 0.0)))
    return to_late, to_early


def level_mask(count, half):
    rows, cols = iota2(count, count, 0), iota2(count, count, 1)
    bits = 2 * half - 1
    return (rows & ~bits) == (cols & ~bits)


def pair_mask(seg_col, seg_row, count):
    same = seg_col == seg_row
    return same & (iota2(count, count, 0) >= iota2(count, count, 1))


def pick_mask(count, offset):
    rows, cols = iota2(count, count, 0), iota2(count, count, 1)
    return cols == ((rows & ~(SUB - 1)) + offset)


def sub_factor(sums3, offset):
    return jnp.exp(jnp.minimum(sums3 - sums3[:, offset : offset + 1, :], 0.0))


def pre_body(
    proj, up3, bias, seg_col, seg_before, logits_o, sums_o, open_o, keep_o, end_o, through_o, pack_o
):
    count = proj.shape[0]
    logits = exact(proj[:, 768:896], up3[...]) + bias[...]
    decay = (jnp.minimum(logits, 0.0) - jnp.log1p(jnp.exp(-jnp.abs(logits)))) / 16.0
    sums = exact(lower(count), decay)
    last = sums[count - 1 : count, :]
    seg = seg_col[...]
    seg_last = seg[count - 1 : count, :]
    before = seg_before[...]
    opened = jnp.where(seg == before, proj[:, 0:128] * jnp.exp(sums), 0.0)
    kept = jnp.where(seg == seg_last, proj[:, 128:256] * jnp.exp(last - sums), 0.0)
    state = exact(proj[:, 256:512], kept, TN)
    through = jnp.where(before == seg_last, jnp.exp(last), 0.0)
    logits_o[...] = logits
    sums_o[...] = sums
    open_o[...] = opened
    keep_o[...] = kept
    end_o[...] = state
    through_o[...] = through
    pack_o[0:VDIM, :] = state.astype(bf16)
    pack_o[VDIM : VDIM + STATE_PAD, :] = jnp.broadcast_to(through, (STATE_PAD, KDIM)).astype(bf16)


def within_body(proj, sums_r, seg_col, seg_row, scores_o, out_o):
    count = proj.shape[0]
    query, key = proj[:, 0:128], proj[:, 128:256]
    sums = sums_r[...]
    scores = jnp.zeros((count, count), f32)
    for half in levels(count):
        to_late, to_early = level_factors(sums, half)
        part = exact(query * to_late, key * to_early, NT)
        scores = scores + jnp.where(level_mask(count, half), part, 0.0)
    blocks = (count // SUB, SUB, KDIM)
    query3, key3, sums3 = query.reshape(blocks), key.reshape(blocks), sums.reshape(blocks)
    for offset in range(SUB):
        weight = sub_factor(sums3, offset)
        column = jnp.sum(query3 * weight * key3[:, offset : offset + 1, :], axis=-1, keepdims=True)
        scores = jnp.where(pick_mask(count, offset), column.reshape(count, 1), scores)
    scores = jnp.where(pair_mask(seg_col[...], seg_row[...], count), scores, 0.0)
    scores_o[...] = scores
    out_o[...] = exact(scores, proj[:, 256:512])


def post_body(within, opened, state_in, proj, gain, unit_o, scale_o, branch_o):
    mixed = within[...] + exact(opened[...], state_in[...], NT)
    scale = lax.rsqrt(jnp.mean(mixed * mixed, axis=-1, keepdims=True) + head_eps)
    unit = mixed * scale
    gate = proj[:, 512:768]
    unit_o[...] = unit
    scale_o[...] = scale
    branch_o[...] = (unit * gain[...] * (gate * jax.nn.sigmoid(gate))).astype(bf16)


def head_back_body(
    branch_delta, unit_r, scale, proj, gain_r, opened, through, low_o, gain_o, mixed_o, pack_o
):
    delta, unit, gate, gain = branch_delta[...], unit_r[...], proj[:, 512:768], gain_r[...]
    sigma = jax.nn.sigmoid(gate)
    swish = gate * sigma
    slope = sigma * (1.0 + gate * (1.0 - sigma))
    low_o[...] = (delta * unit * gain * slope).astype(bf16)
    through_unit = delta * swish
    gain_o[...] = jnp.sum(through_unit * unit, axis=0, keepdims=True)
    inner = through_unit * gain
    mixed = scale[...] * (inner - unit * jnp.mean(inner * unit, axis=-1, keepdims=True))
    mixed_o[...] = mixed
    pack_o[0:VDIM, :] = exact(mixed, opened[...], TN).astype(bf16)
    pack_o[VDIM : VDIM + STATE_PAD, :] = jnp.broadcast_to(
        through[...], (STATE_PAD, KDIM)
    ).astype(bf16)


def within_back_body(
    mixed_r, proj, sums_r, scores, seg_col, seg_row, seg_before, state_in, query_o, key_o, value_o
):
    count = proj.shape[0]
    query, key, value = proj[:, 0:128], proj[:, 128:256], proj[:, 256:512]
    sums, mixed = sums_r[...], mixed_r[...]
    value_o[...] = exact(scores[...], mixed, TN)
    grad = jnp.where(
        pair_mask(seg_col[...], seg_row[...], count), exact(mixed, value, NT), 0.0
    )
    query_delta = jnp.where(
        seg_col[...] == seg_before[...], jnp.exp(sums) * exact(mixed, state_in[...]), 0.0
    )
    key_delta = jnp.zeros((count, KDIM), f32)
    for half in levels(count):
        to_late, to_early = level_factors(sums, half)
        part = jnp.where(level_mask(count, half), grad, 0.0)
        query_delta = query_delta + to_late * exact(part, key * to_early)
        key_delta = key_delta + to_early * exact(part, query * to_late, TN)
    blocks = (count // SUB, SUB, KDIM)
    query3, key3, sums3 = query.reshape(blocks), key.reshape(blocks), sums.reshape(blocks)
    place = lax.broadcasted_iota(jnp.int32, blocks, 1)
    query_sub, key_sub = jnp.zeros(blocks, f32), jnp.zeros(blocks, f32)
    for offset in range(SUB):
        weight = sub_factor(sums3, offset)
        column = jnp.sum(jnp.where(pick_mask(count, offset), grad, 0.0), axis=-1, keepdims=True)
        weighted = weight * column.reshape(count // SUB, SUB, 1)
        query_sub = query_sub + weighted * key3[:, offset : offset + 1, :]
        total = jnp.sum(weighted * query3, axis=1, keepdims=True)
        key_sub = jnp.where(place == offset, total, key_sub)
    query_o[...] = query_delta + query_sub.reshape(count, KDIM)
    key_o[...] = key_delta + key_sub.reshape(count, KDIM)


def state_back_body(
    query_d, key_d, value_d, state_grad, state_in, state_end, through, proj, sums_r, kept,
    logits, seg_col, up3, gate_low, low_o, up_o, bias_o,
):
    count = proj.shape[0]
    grad, sums = state_grad[...], sums_r[...]
    last = sums[count - 1 : count, :]
    seg = seg_col[...]
    query_delta = query_d[...]
    value_delta = value_d[...] + exact(kept[...], grad, NT)
    key_delta = key_d[...] + jnp.where(
        seg == seg[count - 1 : count, :],
        jnp.exp(last - sums) * exact(proj[:, 256:512], grad),
        0.0,
    )
    final = state_end[...] + through[...] * state_in[...]
    beyond = jnp.sum(final * grad, axis=0, keepdims=True)
    local = proj[:, 0:128] * query_delta - proj[:, 128:256] * key_delta
    decay_delta = exact(lower(count), local, TN) + beyond
    logit_delta = decay_delta * jax.nn.sigmoid(-logits[...]) / 16.0
    bias_o[...] = jnp.sum(logit_delta, axis=0, keepdims=True)
    ranks = exact(proj[:, 768:896], logit_delta, TN)
    up_o[...] = ranks[0:16, :] + ranks[16:32, :] + ranks[32:48, :]
    low_o[:, 0:128] = query_delta.astype(bf16)
    low_o[:, 128:256] = key_delta.astype(bf16)
    low_o[:, 256:512] = value_delta.astype(bf16)
    low_o[:, 512:768] = gate_low[...]
    low_o[:, 768:896] = exact(logit_delta, up3[...], NT).astype(bf16)


def scan_states(pack, backward):
    count = lax.axis_size("dp")
    here = lax.axis_index("dp")
    state = pack[:VDIM].astype(f32)
    through = pack[VDIM : VDIM + 1].astype(f32)
    carried, passed = jnp.zeros_like(state), jnp.ones_like(through)
    step = 1
    while step < count:
        other = lax.ppermute(pack, "dp", [(i, i ^ step) for i in range(count)])
        other_state = other[:VDIM].astype(f32)
        other_through = other[VDIM : VDIM + 1].astype(f32)
        mine_later = (here & step) != 0
        ahead = jnp.logical_not(mine_later) if backward else mine_later
        carried = jnp.where(ahead, carried + passed * other_state, carried)
        passed = jnp.where(ahead, passed * other_through, passed)
        state = jnp.where(ahead, state + through * other_state, other_state + other_through * state)
        through = through * other_through
        step *= 2
        if step < count:
            pack = jnp.concatenate(
                [state, jnp.broadcast_to(through, (STATE_PAD, KDIM))], axis=0
            ).astype(bf16)
    return carried


def steps_of(count):
    return [1 << k for k in range(count.bit_length() - 1)]


def butterfly_gather(block, order):
    count, here = lax.axis_size("dp"), lax.axis_index("dp")
    whole, done = block, []
    for step in order:
        other = lax.ppermute(whole, "dp", [(i, i ^ step) for i in range(count)])
        axis = sum(earlier > step for earlier in done)
        late = (here & step) != 0
        whole = jnp.stack(
            [jnp.where(late, other, whole), jnp.where(late, whole, other)], axis=axis
        )
        done.append(step)
    return whole.reshape(count * block.shape[0], block.shape[1])


def butterfly_scatter(grad, order):
    count, here = lax.axis_size("dp"), lax.axis_index("dp")
    left = sorted(order, reverse=True)
    parts = grad.reshape([2] * len(left) + [grad.shape[0] // count, grad.shape[1]])
    for step in order:
        axis = left.index(step)
        low, high = (lax.index_in_dim(parts, k, axis, keepdims=False) for k in range(2))
        late = (here & step) != 0
        got = lax.ppermute(jnp.where(late, low, high), "dp", [(i, i ^ step) for i in range(count)])
        parts = (jnp.where(late, high, low).astype(f32) + got.astype(f32)).astype(bf16)
        left.remove(step)
    return parts


def gather_tokens(block, tensor_index, section_index):
    other = swap(block, "tensor")
    first = tensor_index == 0
    pair = jnp.stack([jnp.where(first, block, other), jnp.where(first, other, block)])
    far = swap(pair, "section")
    left = section_index == 0
    whole = jnp.stack([jnp.where(left, pair, far), jnp.where(left, far, pair)], axis=1)
    return whole.reshape(4 * block.shape[0], block.shape[1])


def scatter_tokens(partial, kind, tensor_index, section_index):
    rows = partial.shape[0] // 4
    parts = partial.reshape(2, 2, rows, partial.shape[1])
    left = section_index == 0
    keep = jnp.where(left, parts[:, 0], parts[:, 1])
    send = jnp.where(left, parts[:, 1], parts[:, 0])
    both = keep + swap(send, "section")
    first = tensor_index == 0
    mine = jnp.where(first, both[0], both[1])
    theirs = jnp.where(first, both[1], both[0]).astype(kind)
    return mine + swap(theirs, "tensor").astype(f32)


def rms_scale(values, epsilon):
    return lax.rsqrt(jnp.mean(values * values, axis=-1, keepdims=True) + epsilon)


def norm_back(grad_unit, unit_values, scale_values):
    return scale_values * (
        grad_unit - unit_values * jnp.mean(grad_unit * unit_values, axis=-1, keepdims=True)
    )


def layer_forward(layer_in, seg, params, where):
    attn, feed, small = params
    mixer_gain, feed_gain, up3, bias, head_gain = small
    seg_col, seg_row, seg_before = seg
    count = seg_col.shape[0]
    scale_one = rms_scale(layer_in, norm_eps)
    hidden_one = gather_tokens((layer_in * scale_one * mixer_gain).astype(bf16), *where)
    proj = mm(hidden_one, attn[:, :896], NN)
    wide, tall = (count, KDIM), (count, VDIM)
    logits, sums, opened, kept, state_end, through, pack = call(
        pre_body,
        [(wide, f32)] * 4
        + [((VDIM, KDIM), f32), ((1, KDIM), f32), ((VDIM + STATE_PAD, KDIM), bf16)],
        proj, up3, bias, seg_col, seg_before,
    )
    scores, within = call(
        within_body, [((count, count), f32), (tall, f32)], proj, sums, seg_col, seg_row
    )
    state_in = scan_states(pack, False)
    unit, scale_head, branch = call(
        post_body,
        [(tall, f32), ((count, 1), f32), (tall, bf16)],
        within, opened, state_in, proj, head_gain,
    )
    mid = layer_in + scatter_tokens(mm(branch, attn[:, 896:], NT), f32, *where)
    scale_two = rms_scale(mid, norm_eps)
    hidden_two = gather_tokens((mid * scale_two * feed_gain).astype(bf16), *where)
    units = feed.shape[1] // 3
    both = mm(hidden_two, feed[:, : 2 * units], NN)
    gate_pre, up_pre = both[:, :units], both[:, units:]
    inner = (jax.nn.silu(gate_pre) * up_pre).astype(bf16)
    result = mid + scatter_tokens(mm(inner, feed[:, 2 * units :], NT), f32, *where)
    saved = (
        layer_in, scale_one, hidden_one, proj, logits, sums, opened, kept, state_end, through,
        scores, state_in, unit, scale_head, branch, mid, scale_two, hidden_two, both, inner,
    )
    return result, saved


def scattered(grad):
    return lax.psum_scatter(grad, "dp", scatter_dimension=0, tiled=True)


def layer_backward(saved, cotangent, seg, params, where, earlier):
    attn, feed, small = params
    mixer_gain, feed_gain, up3, bias, head_gain = small
    seg_col, seg_row, seg_before = seg
    (
        layer_in, scale_one, hidden_one, proj, logits, sums, opened, kept, state_end, through,
        scores, state_in, unit, scale_head, branch, mid, scale_two, hidden_two, both, inner,
    ) = saved
    count = seg_col.shape[0]
    wide, tall = (count, KDIM), (count, VDIM)
    units = feed.shape[1] // 3
    cot = gather_tokens(cotangent.astype(bf16), *where)
    inner_delta = mm(cot, feed[:, 2 * units :], NN)
    gate_pre, up_pre = both[:, :units], both[:, units:]
    sigma = jax.nn.sigmoid(gate_pre)
    gate_delta = inner_delta * up_pre * (sigma * (1.0 + gate_pre * (1.0 - sigma)))
    up_delta = inner_delta * (gate_pre * sigma)
    low_two = jnp.concatenate([gate_delta, up_delta], axis=1).astype(bf16)
    two_delta = mm(low_two, feed[:, : 2 * units], NT)
    feed_grad = jnp.concatenate(
        [mm(hidden_two, low_two, TN).astype(bf16), mm(cot, inner, TN).astype(bf16)],
        axis=1,
    )
    feed_gain_grad = jnp.sum(two_delta * hidden_two.astype(f32), axis=0) / feed_gain
    two_local = scatter_tokens(two_delta, bf16, *where)
    mid_delta = cotangent + norm_back(two_local * feed_gain, mid * scale_two, scale_two)
    mid_delta, feed_grad = lax.optimization_barrier((mid_delta, feed_grad))
    feed_reduced = scattered(feed_grad)
    mid_low = gather_tokens(mid_delta.astype(bf16), *where)
    branch_delta = mm(mid_low, attn[:, 896:], NN)
    gate_low, head_gain_grad, mixed_delta, pack = call(
        head_back_body,
        [(tall, bf16), ((1, VDIM), f32), (tall, f32), ((VDIM + STATE_PAD, KDIM), bf16)],
        branch_delta, unit, scale_head, proj, head_gain, opened, through,
    )
    query_d, key_d, value_d = call(
        within_back_body,
        [(wide, f32), (wide, f32), (tall, f32)],
        mixed_delta, proj, sums, scores, seg_col, seg_row, seg_before, state_in,
    )
    out_grad = mm(mid_low, branch, TN).astype(bf16)
    state_grad = scan_states(pack, True)
    low_one, up_grad, bias_grad = call(
        state_back_body,
        [((count, 896), bf16), ((RANK, KDIM), f32), ((1, KDIM), f32)],
        query_d, key_d, value_d, state_grad, state_in, state_end, through, proj, sums, kept,
        logits, seg_col, up3, gate_low,
    )
    low_one, earlier = lax.optimization_barrier((low_one, earlier))
    one_delta = mm(low_one, attn[:, :896], NT)
    main_grad = mm(hidden_one, low_one, TN)
    mixer_gain_grad = jnp.sum(one_delta * hidden_one.astype(f32), axis=0) / mixer_gain
    depth = main_grad.shape[0]
    tensor_index, section_index = where
    head = tensor_index * 2 + section_index
    ranks = jnp.concatenate([up_grad.T, bias_grad.T, jnp.zeros((KDIM, 1), f32)], axis=1)
    ranks = lax.dynamic_update_slice(
        jnp.zeros((HEADS * KDIM, RANK + 2), f32), ranks, (head * KDIM, 0)
    ).reshape(depth, -1)
    repeat = depth // VDIM
    gains = jnp.broadcast_to(head_gain_grad.reshape(VDIM, 1), (VDIM, repeat)).reshape(depth, 1)
    smalls = jnp.concatenate(
        [main_grad[:, 768:784], mixer_gain_grad[:, None], feed_gain_grad[:, None], ranks, gains],
        axis=1,
    )
    smalls = jnp.pad(smalls, ((0, 0), (0, PACK - smalls.shape[1])))
    attn_grad = (
        main_grad[:, :768].astype(bf16),
        jnp.concatenate([smalls.astype(bf16), out_grad], axis=1),
    )
    one_local = scatter_tokens(one_delta, bf16, *where)
    input_delta = mid_delta + norm_back(one_local * mixer_gain, layer_in * scale_one, scale_one)
    input_delta, attn_grad = lax.optimization_barrier((input_delta, attn_grad))
    return input_delta, attn_grad, feed_reduced, earlier


def in_three(values):
    high = lax.reduce_precision(values, 8, 7)
    rest = values - high
    middle = lax.reduce_precision(rest, 8, 7)
    return [high.astype(bf16), middle.astype(bf16), (rest - middle).astype(bf16)]


def small_params(attn, tensor_index, section_index):
    depth = attn.shape[0]
    pack = attn[:, 768:896].astype(f32)
    rest = pack[:, 48:60] + pack[:, 60:72] + pack[:, 72:84]
    ranks = rest[:, 2:11].reshape(HEADS * KDIM, RANK + 2)
    head = tensor_index * 2 + section_index
    ranks = lax.dynamic_slice_in_dim(ranks, head * KDIM, KDIM, 0).T
    up = ranks[:RANK]
    up3 = jnp.concatenate([up, up, up, jnp.zeros((PACK - 3 * RANK, KDIM), f32)], axis=0)
    head_gain = rest[:, 11].reshape(VDIM, depth // VDIM)[:, 0]
    return rest[:, 0], rest[:, 1], up3, ranks[RANK : RANK + 1], head_gain[None]


def shards(
    inputs, segments, mixer_gain, query_weight, key_weight, value_weight, outgate_weight,
    decay_down, decay_up, decay_bias, head_gain, output_weight, feed_gain, gate_weight,
    up_weight, down_weight, cotangent,
):
    section_index = lax.axis_index("section")
    tensor_index = lax.axis_index("tensor")
    dp_index = lax.axis_index("dp")
    where = (tensor_index, section_index)
    left, first = section_index == 0, tensor_index == 0
    segment_ids = segments.astype(f32)
    count = segment_ids.shape[0]

    narrow = mixer_gain.shape[1]
    ranks = jnp.concatenate(
        [decay_up[0].T, decay_bias[0][:, None], jnp.zeros((decay_bias.shape[1], 1), f32)], axis=1
    ).reshape(narrow, -1)
    spread = narrow // head_gain.shape[1]
    gains = jnp.broadcast_to(head_gain[0][:, None], (head_gain.shape[1], spread)).reshape(narrow, 1)
    mine = jnp.concatenate(
        [decay_down[0], mixer_gain[0][:, None], feed_gain[0][:, None], ranks, gains], axis=1
    )
    theirs = swap(mine, "tensor")
    rows = jnp.concatenate([jnp.where(first, mine, theirs), jnp.where(first, theirs, mine)], axis=0)
    seg_end = jnp.broadcast_to(segment_ids[-1:][None], (2 * narrow, 1)).astype(bf16)
    pack = jnp.concatenate(in_three(rows[:, :RANK]) + in_three(rows[:, RANK:]) + [seg_end], axis=1)
    pack = jnp.pad(pack, ((0, 0), (0, PACK - pack.shape[1])))

    def half(weight, side):
        width = weight.shape[1] // 2
        return weight[:, side * width : (side + 1) * width]

    out_t, down_t = output_weight[0].T, down_weight[0].T

    def attn_half(side):
        parts = [half(w, side) for w in (query_weight[0], key_weight[0], value_weight[0], outgate_weight[0])]
        return jnp.concatenate(parts + [pack, half(out_t, side)], axis=1)

    def feed_half(side):
        parts = [half(w, side) for w in (gate_weight[0], up_weight[0], down_t)]
        return jnp.concatenate(parts, axis=1)

    def per_layer(side_zero, side_one):
        keep = jnp.where(left, side_zero, side_one)
        got = swap(jnp.where(left, side_one, side_zero), "section")
        return jnp.where(left, keep, got), jnp.where(left, got, keep)

    attn_parts = per_layer(attn_half(0), attn_half(1))
    feed_parts = per_layer(feed_half(0), feed_half(1))

    def gathered(part):
        return lax.all_gather(part, "dp", axis=0, tiled=True)

    attn_width = attn_parts[0].shape[1]
    near_first = steps_of(lax.axis_size("dp"))
    far_first = near_first[::-1]
    cut = 640
    attn0 = jnp.concatenate(
        [
            butterfly_gather(attn_parts[0][:, :cut], far_first),
            butterfly_gather(attn_parts[0][:, cut:], near_first),
        ],
        axis=1,
    )
    middle = gathered(jnp.concatenate([attn_parts[1], feed_parts[0]], axis=1))
    feed1 = gathered(feed_parts[1])
    wide = 2 * narrow
    earlier = lax.dynamic_slice(
        attn0, (jnp.maximum(dp_index - 1, 0) * wide, 768 + 84), (1, 1)
    ).astype(f32)
    seg_before = jnp.where(dp_index == 0, -1.0, earlier)
    seg = (segment_ids[:, None], segment_ids[None, :], seg_before)

    own = inputs.shape[0] // 2
    layer_in = lax.dynamic_slice_in_dim(inputs, section_index * own, own, 0)
    cot = lax.dynamic_slice_in_dim(cotangent, section_index * own, own, 0)
    params0 = (attn0, middle[:, attn_width:], small_params(attn0, *where))
    out0, saved0 = layer_forward(layer_in, seg, params0, where)
    late, out0 = lax.optimization_barrier((middle, out0))
    attn1 = late[:, :attn_width]
    params1 = (attn1, feed1, small_params(attn1, *where))
    out1, saved1 = layer_forward(out0, seg, params1, where)
    delta1, attn_grad1, feed_red1, _ = layer_backward(saved1, cot, seg, params1, where, [])

    def attn_reduced(grad):
        orders = (near_first, far_first)
        return [butterfly_scatter(part, order) for part, order in zip(grad, orders)]

    attn_red1 = attn_reduced(attn_grad1)
    delta0, attn_grad0, feed_red0, earlier = layer_backward(
        saved0, delta1, seg, params0, where, [feed_red1, attn_red1]
    )
    feed_red1, attn_red1 = earlier
    attn_red0 = attn_reduced(attn_grad0)
    attn_red0, attn_red1 = (jnp.concatenate(red, axis=1) for red in (attn_red0, attn_red1))

    def to_section(of_zero, of_one):
        keep = jnp.where(left, of_zero, of_one)
        got = swap(jnp.where(left, of_one, of_zero), "section")
        return keep, got

    def joined(keep, got, axis):
        return jnp.concatenate([jnp.where(left, keep, got), jnp.where(left, got, keep)], axis=axis)

    section_out = joined(*to_section(out0, out1), 0)
    input_grad = joined(*to_section(delta0, delta1), 0)
    attn_keep, attn_got = to_section(attn_red0, attn_red1)
    feed_keep, feed_got = to_section(feed_red0, feed_red1)

    def columns(keep, got, start, width):
        return joined(keep[:, start : start + width], got[:, start : start + width], 1).astype(f32)

    units = feed_keep.shape[1] // 3
    small = attn_keep[:, 768:896].astype(f32) + attn_got[:, 768:896].astype(f32)
    small_mine = jnp.where(first, small[:narrow], small[narrow:])
    small_theirs = jnp.where(first, small[narrow:], small[:narrow])
    small = small_mine + swap(small_theirs, "tensor")
    ranks = small[:, 18:27].reshape(decay_bias.shape[1], RANK + 2)
    outs = (
        section_out,
        input_grad,
        small[:, 16],
        columns(attn_keep, attn_got, 0, 128),
        columns(attn_keep, attn_got, 128, 128),
        columns(attn_keep, attn_got, 256, 256),
        columns(attn_keep, attn_got, 512, 256),
        small[:, :16],
        ranks[:, :RANK].T,
        ranks[:, RANK],
        small[:, 27].reshape(-1, spread)[:, 0],
        columns(attn_keep, attn_got, 896, 256).T,
        small[:, 17],
        columns(feed_keep, feed_got, 0, units),
        columns(feed_keep, feed_got, units, units),
        columns(feed_keep, feed_got, 2 * units, units).T,
    )
    return tuple(out[None] for out in outs)


def solution(mesh):
    rows = P(("dp", "tensor"), None)
    vector = P("section", ("dp", "tensor"))
    down_in = P("section", "dp", "tensor")
    up_out = P("section", "tensor", "dp")
    placed = (
        rows, P("dp"), vector, down_in, down_in, down_in, down_in,
        P("section", ("dp", "tensor"), None), P("section", None, ("dp", "tensor")),
        vector, vector, up_out, vector, down_in, down_in, up_out, rows,
    )
    tokens = P("section", ("dp", "tensor"), None)
    return jax.shard_map(
        shards,
        mesh=mesh,
        in_specs=placed,
        out_specs=(
            tokens, tokens, vector, down_in, down_in, down_in, down_in, tokens,
            P("section", None, ("dp", "tensor")), vector, vector, up_out, vector,
            down_in, down_in, up_out,
        ),
        check_vma=False,
    )
```

```python
import functools

import jax
import jax.numpy as jnp
from jax import lax
from jax.experimental import pallas as pl
from jax.experimental.layout import Layout, with_layout_constraint
from jax.experimental.pallas import tpu as pltpu
from jax.sharding import PartitionSpec as P

HEADS = 4
KDIM = 128
VDIM = 256
RANK = 16
SUB = 16
PACK = 128
STATE_PAD = 16

norm_eps = 1e-06
head_eps = 1e-05
f32 = jnp.float32
bf16 = jnp.bfloat16
INTERPRET = False


def row_major(block):
    return with_layout_constraint(block, Layout(major_to_minor=tuple(range(block.ndim))))


def swap(block, axis):
    return lax.ppermute(block, axis, [(0, 1), (1, 0)])


def mm(left, right, dims):
    return lax.dot_general(left, right, (dims, ((), ())), preferred_element_type=f32)


def exact(left, right, dims=((1,), (0,))):
    return lax.dot_general(
        left, right, (dims, ((), ())), precision=lax.Precision.HIGHEST, preferred_element_type=f32
    )


NN = ((1,), (0,))
NT = ((1,), (1,))
TN = ((0,), (0,))


def call(body, outs, *args):
    return pl.pallas_call(
        body,
        out_shape=[jax.ShapeDtypeStruct(shape, kind) for shape, kind in outs],
        interpret=INTERPRET,
    )(*args)


def iota2(rows, cols, axis):
    return lax.broadcasted_iota(jnp.int32, (rows, cols), axis)


def lower(count):
    return jnp.where(iota2(count, count, 0) >= iota2(count, count, 1), 1.0, 0.0)


def levels(count):
    half, out = count // 2, []
    while half >= SUB:
        out.append(half)
        half //= 2
    return out


def level_factors(sums, half):
    count, width = sums.shape
    parts = sums.reshape(count // (2 * half), 2 * half, width)
    middle = jnp.broadcast_to(parts[:, half - 1 : half, :], parts.shape).reshape(count, width)
    late = (iota2(count, width, 0) & half) != 0
    gap = sums - middle
    to_late = jnp.where(late, jnp.exp(jnp.minimum(gap, 0.0)), 0.0)
    to_early = jnp.where(late, 0.0, jnp.exp(jnp.minimum(-gap, 0.0)))
    return to_late, to_early


def level_mask(count, half):
    rows, cols = iota2(count, count, 0), iota2(count, count, 1)
    bits = 2 * half - 1
    return (rows & ~bits) == (cols & ~bits)


def pair_mask(seg_col, seg_row, count):
    same = seg_col == seg_row
    return same & (iota2(count, count, 0) >= iota2(count, count, 1))


def pick_mask(count, offset):
    rows, cols = iota2(count, count, 0), iota2(count, count, 1)
    return cols == ((rows & ~(SUB - 1)) + offset)


def sub_factor(sums3, offset):
    return jnp.exp(jnp.minimum(sums3 - sums3[:, offset : offset + 1, :], 0.0))


def pre_body(
    proj, up3, bias, seg_col, seg_before, logits_o, sums_o, open_o, keep_o, end_o, through_o, pack_o
):
    count = proj.shape[0]
    logits = exact(proj[:, 768:896], up3[...]) + bias[...]
    decay = (jnp.minimum(logits, 0.0) - jnp.log1p(jnp.exp(-jnp.abs(logits)))) / 16.0
    sums = exact(lower(count), decay)
    last = sums[count - 1 : count, :]
    seg = seg_col[...]
    seg_last = seg[count - 1 : count, :]
    before = seg_before[...]
    opened = jnp.where(seg == before, proj[:, 0:128] * jnp.exp(sums), 0.0)
    kept = jnp.where(seg == seg_last, proj[:, 128:256] * jnp.exp(last - sums), 0.0)
    state = exact(proj[:, 256:512], kept, TN)
    through = jnp.where(before == seg_last, jnp.exp(last), 0.0)
    logits_o[...] = logits
    sums_o[...] = sums
    open_o[...] = opened
    keep_o[...] = kept
    end_o[...] = state
    through_o[...] = through
    pack_o[0:VDIM, :] = state.astype(bf16)
    pack_o[VDIM : VDIM + STATE_PAD, :] = jnp.broadcast_to(through, (STATE_PAD, KDIM)).astype(bf16)


def within_body(proj, sums_r, seg_col, seg_row, scores_o, out_o):
    count = proj.shape[0]
    query, key = proj[:, 0:128], proj[:, 128:256]
    sums = sums_r[...]
    scores = jnp.zeros((count, count), f32)
    for half in levels(count):
        to_late, to_early = level_factors(sums, half)
        part = exact(query * to_late, key * to_early, NT)
        scores = scores + jnp.where(level_mask(count, half), part, 0.0)
    blocks = (count // SUB, SUB, KDIM)
    query3, key3, sums3 = query.reshape(blocks), key.reshape(blocks), sums.reshape(blocks)
    for offset in range(SUB):
        weight = sub_factor(sums3, offset)
        column = jnp.sum(query3 * weight * key3[:, offset : offset + 1, :], axis=-1, keepdims=True)
        scores = jnp.where(pick_mask(count, offset), column.reshape(count, 1), scores)
    scores = jnp.where(pair_mask(seg_col[...], seg_row[...], count), scores, 0.0)
    scores_o[...] = scores
    out_o[...] = exact(scores, proj[:, 256:512])


def post_body(within, opened, state_in, proj, gain, unit_o, scale_o, branch_o):
    mixed = within[...] + exact(opened[...], state_in[...], NT)
    scale = lax.rsqrt(jnp.mean(mixed * mixed, axis=-1, keepdims=True) + head_eps)
    unit = mixed * scale
    gate = proj[:, 512:768]
    unit_o[...] = unit
    scale_o[...] = scale
    branch_o[...] = (unit * gain[...] * (gate * jax.nn.sigmoid(gate))).astype(bf16)


def head_back_body(
    branch_delta, unit_r, scale, proj, gain_r, opened, through, low_o, gain_o, mixed_o, pack_o
):
    delta, unit, gate, gain = branch_delta[...], unit_r[...], proj[:, 512:768], gain_r[...]
    sigma = jax.nn.sigmoid(gate)
    swish = gate * sigma
    slope = sigma * (1.0 + gate * (1.0 - sigma))
    low_o[...] = (delta * unit * gain * slope).astype(bf16)
    through_unit = delta * swish
    gain_o[...] = jnp.sum(through_unit * unit, axis=0, keepdims=True)
    inner = through_unit * gain
    mixed = scale[...] * (inner - unit * jnp.mean(inner * unit, axis=-1, keepdims=True))
    mixed_o[...] = mixed
    pack_o[0:VDIM, :] = exact(mixed, opened[...], TN).astype(bf16)
    pack_o[VDIM : VDIM + STATE_PAD, :] = jnp.broadcast_to(
        through[...], (STATE_PAD, KDIM)
    ).astype(bf16)


def within_back_body(
    mixed_r, proj, sums_r, scores, seg_col, seg_row, seg_before, state_in, query_o, key_o, value_o
):
    count = proj.shape[0]
    query, key, value = proj[:, 0:128], proj[:, 128:256], proj[:, 256:512]
    sums, mixed = sums_r[...], mixed_r[...]
    value_o[...] = exact(scores[...], mixed, TN)
    grad = jnp.where(
        pair_mask(seg_col[...], seg_row[...], count), exact(mixed, value, NT), 0.0
    )
    query_delta = jnp.where(
        seg_col[...] == seg_before[...], jnp.exp(sums) * exact(mixed, state_in[...]), 0.0
    )
    key_delta = jnp.zeros((count, KDIM), f32)
    for half in levels(count):
        to_late, to_early = level_factors(sums, half)
        part = jnp.where(level_mask(count, half), grad, 0.0)
        query_delta = query_delta + to_late * exact(part, key * to_early)
        key_delta = key_delta + to_early * exact(part, query * to_late, TN)
    blocks = (count // SUB, SUB, KDIM)
    query3, key3, sums3 = query.reshape(blocks), key.reshape(blocks), sums.reshape(blocks)
    place = lax.broadcasted_iota(jnp.int32, blocks, 1)
    query_sub, key_sub = jnp.zeros(blocks, f32), jnp.zeros(blocks, f32)
    for offset in range(SUB):
        weight = sub_factor(sums3, offset)
        column = jnp.sum(jnp.where(pick_mask(count, offset), grad, 0.0), axis=-1, keepdims=True)
        weighted = weight * column.reshape(count // SUB, SUB, 1)
        query_sub = query_sub + weighted * key3[:, offset : offset + 1, :]
        total = jnp.sum(weighted * query3, axis=1, keepdims=True)
        key_sub = jnp.where(place == offset, total, key_sub)
    query_o[...] = query_delta + query_sub.reshape(count, KDIM)
    key_o[...] = key_delta + key_sub.reshape(count, KDIM)


def state_back_body(
    query_d, key_d, value_d, state_grad, state_in, state_end, through, proj, sums_r, kept,
    logits, seg_col, up3, gate_low, low_o, up_o, bias_o,
):
    count = proj.shape[0]
    grad, sums = state_grad[...], sums_r[...]
    last = sums[count - 1 : count, :]
    seg = seg_col[...]
    query_delta = query_d[...]
    value_delta = value_d[...] + exact(kept[...], grad, NT)
    key_delta = key_d[...] + jnp.where(
        seg == seg[count - 1 : count, :],
        jnp.exp(last - sums) * exact(proj[:, 256:512], grad),
        0.0,
    )
    final = state_end[...] + through[...] * state_in[...]
    beyond = jnp.sum(final * grad, axis=0, keepdims=True)
    local = proj[:, 0:128] * query_delta - proj[:, 128:256] * key_delta
    decay_delta = exact(lower(count), local, TN) + beyond
    logit_delta = decay_delta * jax.nn.sigmoid(-logits[...]) / 16.0
    bias_o[...] = jnp.sum(logit_delta, axis=0, keepdims=True)
    ranks = exact(proj[:, 768:896], logit_delta, TN)
    up_o[...] = ranks[0:16, :] + ranks[16:32, :] + ranks[32:48, :]
    low_o[:, 0:128] = query_delta.astype(bf16)
    low_o[:, 128:256] = key_delta.astype(bf16)
    low_o[:, 256:512] = value_delta.astype(bf16)
    low_o[:, 512:768] = gate_low[...]
    low_o[:, 768:896] = exact(logit_delta, up3[...], NT).astype(bf16)


def scan_states(pack, backward):
    count = lax.axis_size("dp")
    here = lax.axis_index("dp")
    state = pack[:VDIM].astype(f32)
    through = pack[VDIM : VDIM + 1].astype(f32)
    carried, passed = jnp.zeros_like(state), jnp.ones_like(through)
    step = 1
    while step < count:
        other = lax.ppermute(pack, "dp", [(i, i ^ step) for i in range(count)])
        other_state = other[:VDIM].astype(f32)
        other_through = other[VDIM : VDIM + 1].astype(f32)
        mine_later = (here & step) != 0
        ahead = jnp.logical_not(mine_later) if backward else mine_later
        carried = jnp.where(ahead, carried + passed * other_state, carried)
        passed = jnp.where(ahead, passed * other_through, passed)
        state = jnp.where(ahead, state + through * other_state, other_state + other_through * state)
        through = through * other_through
        step *= 2
        if step < count:
            pack = jnp.concatenate(
                [state, jnp.broadcast_to(through, (STATE_PAD, KDIM))], axis=0
            ).astype(bf16)
    return carried


def steps_of(count):
    return [1 << k for k in range(count.bit_length() - 1)]


def butterfly_gather(block, order):
    count, here = lax.axis_size("dp"), lax.axis_index("dp")
    whole, done = block, []
    for step in order:
        other = lax.ppermute(row_major(whole), "dp", [(i, i ^ step) for i in range(count)])
        axis = sum(earlier > step for earlier in done)
        late = (here & step) != 0
        whole = jnp.stack(
            [jnp.where(late, other, whole), jnp.where(late, whole, other)], axis=axis
        )
        done.append(step)
    return whole.reshape(count * block.shape[0], block.shape[1])


def butterfly_scatter(grad, order):
    count, here = lax.axis_size("dp"), lax.axis_index("dp")
    left = sorted(order, reverse=True)
    parts = grad.reshape([2] * len(left) + [grad.shape[0] // count, grad.shape[1]])
    for step in order:
        axis = left.index(step)
        low, high = (lax.index_in_dim(parts, k, axis, keepdims=False) for k in range(2))
        late = (here & step) != 0
        send = row_major(jnp.where(late, low, high))
        got = row_major(lax.ppermute(send, "dp", [(i, i ^ step) for i in range(count)]))
        parts = (jnp.where(late, high, low).astype(f32) + got.astype(f32)).astype(bf16)
        left.remove(step)
    return parts


def gather_tokens(block, tensor_index, section_index):
    other = swap(block, "tensor")
    first = tensor_index == 0
    pair = jnp.stack([jnp.where(first, block, other), jnp.where(first, other, block)])
    far = swap(pair, "section")
    left = section_index == 0
    whole = jnp.stack([jnp.where(left, pair, far), jnp.where(left, far, pair)], axis=1)
    return whole.reshape(4 * block.shape[0], block.shape[1])


def scatter_tokens(partial, kind, tensor_index, section_index):
    rows = partial.shape[0] // 4
    parts = partial.reshape(2, 2, rows, partial.shape[1])
    left = section_index == 0
    keep = jnp.where(left, parts[:, 0], parts[:, 1])
    send = jnp.where(left, parts[:, 1], parts[:, 0])
    both = keep + swap(send, "section")
    first = tensor_index == 0
    mine = jnp.where(first, both[0], both[1])
    theirs = jnp.where(first, both[1], both[0]).astype(kind)
    return mine + swap(theirs, "tensor").astype(f32)


def rms_scale(values, epsilon):
    return lax.rsqrt(jnp.mean(values * values, axis=-1, keepdims=True) + epsilon)


def norm_back(grad_unit, unit_values, scale_values):
    return scale_values * (
        grad_unit - unit_values * jnp.mean(grad_unit * unit_values, axis=-1, keepdims=True)
    )


def layer_forward(layer_in, seg, params, where):
    attn, feed, small = params
    mixer_gain, feed_gain, up3, bias, head_gain = small
    seg_col, seg_row, seg_before = seg
    count = seg_col.shape[0]
    scale_one = rms_scale(layer_in, norm_eps)
    hidden_one = gather_tokens((layer_in * scale_one * mixer_gain).astype(bf16), *where)
    proj = mm(hidden_one, attn[:, :896], NN)
    wide, tall = (count, KDIM), (count, VDIM)
    logits, sums, opened, kept, state_end, through, pack = call(
        pre_body,
        [(wide, f32)] * 4
        + [((VDIM, KDIM), f32), ((1, KDIM), f32), ((VDIM + STATE_PAD, KDIM), bf16)],
        proj, up3, bias, seg_col, seg_before,
    )
    scores, within = call(
        within_body, [((count, count), f32), (tall, f32)], proj, sums, seg_col, seg_row
    )
    state_in = scan_states(pack, False)
    unit, scale_head, branch = call(
        post_body,
        [(tall, f32), ((count, 1), f32), (tall, bf16)],
        within, opened, state_in, proj, head_gain,
    )
    mid = layer_in + scatter_tokens(mm(branch, attn[:, 896:], NT), f32, *where)
    scale_two = rms_scale(mid, norm_eps)
    hidden_two = gather_tokens((mid * scale_two * feed_gain).astype(bf16), *where)
    units = feed.shape[1] // 3
    both = mm(hidden_two, feed[:, : 2 * units], NN)
    gate_pre, up_pre = both[:, :units], both[:, units:]
    inner = (jax.nn.silu(gate_pre) * up_pre).astype(bf16)
    result = mid + scatter_tokens(mm(inner, feed[:, 2 * units :], NT), f32, *where)
    saved = (
        layer_in, scale_one, hidden_one, proj, logits, sums, opened, kept, state_end, through,
        scores, state_in, unit, scale_head, branch, mid, scale_two, hidden_two, both, inner,
    )
    return result, saved


def scattered(grad):
    return lax.psum_scatter(grad, "dp", scatter_dimension=0, tiled=True)


def layer_backward(saved, cotangent, seg, params, where, pending, earlier):
    attn, feed, small = params
    mixer_gain, feed_gain, up3, bias, head_gain = small
    seg_col, seg_row, seg_before = seg
    (
        layer_in, scale_one, hidden_one, proj, logits, sums, opened, kept, state_end, through,
        scores, state_in, unit, scale_head, branch, mid, scale_two, hidden_two, both, inner,
    ) = saved
    count = seg_col.shape[0]
    wide, tall = (count, KDIM), (count, VDIM)
    units = feed.shape[1] // 3
    cot = gather_tokens(cotangent.astype(bf16), *where)
    inner_delta = mm(cot, feed[:, 2 * units :], NN)
    gate_pre, up_pre = both[:, :units], both[:, units:]
    sigma = jax.nn.sigmoid(gate_pre)
    gate_delta = inner_delta * up_pre * (sigma * (1.0 + gate_pre * (1.0 - sigma)))
    up_delta = inner_delta * (gate_pre * sigma)
    low_two = jnp.concatenate([gate_delta, up_delta], axis=1).astype(bf16)
    two_delta = mm(low_two, feed[:, : 2 * units], NT)
    feed_grad = jnp.concatenate(
        pending + [mm(hidden_two, low_two, TN).astype(bf16), mm(cot, inner, TN).astype(bf16)],
        axis=1,
    )
    feed_gain_grad = jnp.sum(two_delta * hidden_two.astype(f32), axis=0) / feed_gain
    two_local = scatter_tokens(two_delta, bf16, *where)
    mid_delta = cotangent + norm_back(two_local * feed_gain, mid * scale_two, scale_two)
    mid_delta, feed_grad = lax.optimization_barrier((mid_delta, feed_grad))
    feed_reduced = scattered(feed_grad)
    mid_low = gather_tokens(mid_delta.astype(bf16), *where)
    branch_delta = mm(mid_low, attn[:, 896:], NN)
    gate_low, head_gain_grad, mixed_delta, pack = call(
        head_back_body,
        [(tall, bf16), ((1, VDIM), f32), (tall, f32), ((VDIM + STATE_PAD, KDIM), bf16)],
        branch_delta, unit, scale_head, proj, head_gain, opened, through,
    )
    query_d, key_d, value_d = call(
        within_back_body,
        [(wide, f32), (wide, f32), (tall, f32)],
        mixed_delta, proj, sums, scores, seg_col, seg_row, seg_before, state_in,
    )
    out_grad = mm(mid_low, branch, TN).astype(bf16)
    state_grad = scan_states(pack, True)
    low_one, up_grad, bias_grad = call(
        state_back_body,
        [((count, 896), bf16), ((RANK, KDIM), f32), ((1, KDIM), f32)],
        query_d, key_d, value_d, state_grad, state_in, state_end, through, proj, sums, kept,
        logits, seg_col, up3, gate_low,
    )
    low_one, earlier = lax.optimization_barrier((low_one, earlier))
    one_delta = mm(low_one, attn[:, :896], NT)
    main_grad = mm(hidden_one, low_one, TN)
    mixer_gain_grad = jnp.sum(one_delta * hidden_one.astype(f32), axis=0) / mixer_gain
    depth = main_grad.shape[0]
    tensor_index, section_index = where
    head = tensor_index * 2 + section_index
    ranks = jnp.concatenate([up_grad.T, bias_grad.T, jnp.zeros((KDIM, 1), f32)], axis=1)
    ranks = lax.dynamic_update_slice(
        jnp.zeros((HEADS * KDIM, RANK + 2), f32), ranks, (head * KDIM, 0)
    ).reshape(depth, -1)
    repeat = depth // VDIM
    gains = jnp.broadcast_to(head_gain_grad.reshape(VDIM, 1), (VDIM, repeat)).reshape(depth, 1)
    smalls = jnp.concatenate(
        [main_grad[:, 768:784], mixer_gain_grad[:, None], feed_gain_grad[:, None], ranks, gains],
        axis=1,
    )
    smalls = jnp.pad(smalls, ((0, 0), (0, PACK - smalls.shape[1])))
    attn_grad = (
        main_grad[:, :768].astype(bf16),
        jnp.concatenate([smalls.astype(bf16), out_grad], axis=1),
    )
    one_local = scatter_tokens(one_delta, bf16, *where)
    input_delta = mid_delta + norm_back(one_local * mixer_gain, layer_in * scale_one, scale_one)
    input_delta, attn_grad = lax.optimization_barrier((input_delta, attn_grad))
    return input_delta, attn_grad, feed_reduced, earlier


def in_three(values):
    high = lax.reduce_precision(values, 8, 7)
    rest = values - high
    middle = lax.reduce_precision(rest, 8, 7)
    return [high.astype(bf16), middle.astype(bf16), (rest - middle).astype(bf16)]


def small_params(attn, tensor_index, section_index):
    depth = attn.shape[0]
    pack = attn[:, 768:896].astype(f32)
    rest = pack[:, 48:60] + pack[:, 60:72] + pack[:, 72:84]
    ranks = rest[:, 2:11].reshape(HEADS * KDIM, RANK + 2)
    head = tensor_index * 2 + section_index
    ranks = lax.dynamic_slice_in_dim(ranks, head * KDIM, KDIM, 0).T
    up = ranks[:RANK]
    up3 = jnp.concatenate([up, up, up, jnp.zeros((PACK - 3 * RANK, KDIM), f32)], axis=0)
    head_gain = rest[:, 11].reshape(VDIM, depth // VDIM)[:, 0]
    return rest[:, 0], rest[:, 1], up3, ranks[RANK : RANK + 1], head_gain[None]


def shards(
    inputs, segments, mixer_gain, query_weight, key_weight, value_weight, outgate_weight,
    decay_down, decay_up, decay_bias, head_gain, output_weight, feed_gain, gate_weight,
    up_weight, down_weight, cotangent,
):
    section_index = lax.axis_index("section")
    tensor_index = lax.axis_index("tensor")
    dp_index = lax.axis_index("dp")
    where = (tensor_index, section_index)
    left, first = section_index == 0, tensor_index == 0
    segment_ids = segments.astype(f32)
    count = segment_ids.shape[0]

    narrow = mixer_gain.shape[1]
    ranks = jnp.concatenate(
        [decay_up[0].T, decay_bias[0][:, None], jnp.zeros((decay_bias.shape[1], 1), f32)], axis=1
    ).reshape(narrow, -1)
    spread = narrow // head_gain.shape[1]
    gains = jnp.broadcast_to(head_gain[0][:, None], (head_gain.shape[1], spread)).reshape(narrow, 1)
    mine = jnp.concatenate(
        [decay_down[0], mixer_gain[0][:, None], feed_gain[0][:, None], ranks, gains], axis=1
    )
    theirs = swap(mine, "tensor")
    rows = jnp.concatenate([jnp.where(first, mine, theirs), jnp.where(first, theirs, mine)], axis=0)
    seg_end = jnp.broadcast_to(segment_ids[-1:][None], (2 * narrow, 1)).astype(bf16)
    pack = jnp.concatenate(in_three(rows[:, :RANK]) + in_three(rows[:, RANK:]) + [seg_end], axis=1)
    pack = jnp.pad(pack, ((0, 0), (0, PACK - pack.shape[1])))

    def half(weight, side):
        width = weight.shape[1] // 2
        return weight[:, side * width : (side + 1) * width]

    out_t, down_t = output_weight[0].T, down_weight[0].T

    def attn_half(side):
        parts = [half(w, side) for w in (query_weight[0], key_weight[0], value_weight[0], outgate_weight[0])]
        return jnp.concatenate(parts + [pack, half(out_t, side)], axis=1)

    def feed_half(side):
        parts = [half(w, side) for w in (gate_weight[0], up_weight[0], down_t)]
        return jnp.concatenate(parts, axis=1)

    def per_layer(side_zero, side_one):
        keep = jnp.where(left, side_zero, side_one)
        got = row_major(swap(row_major(jnp.where(left, side_one, side_zero)), "section"))
        return jnp.where(left, keep, got), jnp.where(left, got, keep)

    attn_parts = per_layer(attn_half(0), attn_half(1))
    feed_parts = per_layer(feed_half(0), feed_half(1))

    def gathered(part):
        return lax.all_gather(row_major(part), "dp", axis=0, tiled=True)

    attn_width = attn_parts[0].shape[1]
    near_first = steps_of(lax.axis_size("dp"))
    far_first = near_first[::-1]
    cut = 640
    attn0 = jnp.concatenate(
        [
            butterfly_gather(attn_parts[0][:, :cut], far_first),
            butterfly_gather(attn_parts[0][:, cut:], near_first),
        ],
        axis=1,
    )
    middle = gathered(jnp.concatenate([attn_parts[1], feed_parts[0]], axis=1))
    feed1 = gathered(feed_parts[1])
    wide = 2 * narrow
    earlier = lax.dynamic_slice(
        attn0, (jnp.maximum(dp_index - 1, 0) * wide, 768 + 84), (1, 1)
    ).astype(f32)
    seg_before = jnp.where(dp_index == 0, -1.0, earlier)
    seg = (segment_ids[:, None], segment_ids[None, :], seg_before)

    own = inputs.shape[0] // 2
    layer_in = lax.dynamic_slice_in_dim(inputs, section_index * own, own, 0)
    cot = lax.dynamic_slice_in_dim(cotangent, section_index * own, own, 0)
    params0 = (attn0, middle[:, attn_width:], small_params(attn0, *where))
    out0, saved0 = layer_forward(layer_in, seg, params0, where)
    late, out0 = lax.optimization_barrier((middle, out0))
    attn1 = late[:, :attn_width]
    params1 = (attn1, feed1, small_params(attn1, *where))
    out1, saved1 = layer_forward(out0, seg, params1, where)
    delta1, attn_grad1, feed_red1, _ = layer_backward(saved1, cot, seg, params1, where, [], [])
    delta0, attn_grad0, mixed_red, (feed_red1,) = layer_backward(
        saved0, delta1, seg, params0, where, list(attn_grad1), [feed_red1]
    )
    attn_red0 = jnp.concatenate(
        [
            butterfly_scatter(attn_grad0[0], near_first),
            butterfly_scatter(attn_grad0[1], far_first),
        ],
        axis=1,
    )
    mixed_red, attn_red0 = lax.optimization_barrier((mixed_red, attn_red0))
    attn_red1, feed_red0 = mixed_red[:, :attn_width], mixed_red[:, attn_width:]

    def to_section(of_zero, of_one):
        keep = jnp.where(left, of_zero, of_one)
        got = swap(jnp.where(left, of_one, of_zero), "section")
        return keep, got

    def joined(keep, got, axis):
        return jnp.concatenate([jnp.where(left, keep, got), jnp.where(left, got, keep)], axis=axis)

    section_out = joined(*to_section(out0, out1), 0)
    input_grad = joined(*to_section(delta0, delta1), 0)
    attn_keep, attn_got = to_section(attn_red0, attn_red1)
    feed_keep, feed_got = to_section(feed_red0, feed_red1)

    def columns(keep, got, start, width):
        return joined(keep[:, start : start + width], got[:, start : start + width], 1).astype(f32)

    units = feed_keep.shape[1] // 3
    small = attn_keep[:, 768:896].astype(f32) + attn_got[:, 768:896].astype(f32)
    small_mine = jnp.where(first, small[:narrow], small[narrow:])
    small_theirs = jnp.where(first, small[narrow:], small[:narrow])
    small = small_mine + swap(small_theirs, "tensor")
    ranks = small[:, 18:27].reshape(decay_bias.shape[1], RANK + 2)
    outs = (
        section_out,
        input_grad,
        small[:, 16],
        columns(attn_keep, attn_got, 0, 128),
        columns(attn_keep, attn_got, 128, 128),
        columns(attn_keep, attn_got, 256, 256),
        columns(attn_keep, attn_got, 512, 256),
        small[:, :16],
        ranks[:, :RANK].T,
        ranks[:, RANK],
        small[:, 27].reshape(-1, spread)[:, 0],
        columns(attn_keep, attn_got, 896, 256).T,
        small[:, 17],
        columns(feed_keep, feed_got, 0, units),
        columns(feed_keep, feed_got, units, units),
        columns(feed_keep, feed_got, 2 * units, units).T,
    )
    return tuple(out[None] for out in outs)


def solution(mesh):
    rows = P(("dp", "tensor"), None)
    vector = P("section", ("dp", "tensor"))
    down_in = P("section", "dp", "tensor")
    up_out = P("section", "tensor", "dp")
    placed = (
        rows, P("dp"), vector, down_in, down_in, down_in, down_in,
        P("section", ("dp", "tensor"), None), P("section", None, ("dp", "tensor")),
        vector, vector, up_out, vector, down_in, down_in, up_out, rows,
    )
    tokens = P("section", ("dp", "tensor"), None)
    return jax.shard_map(
        shards,
        mesh=mesh,
        in_specs=placed,
        out_specs=(
            tokens, tokens, vector, down_in, down_in, down_in, down_in, tokens,
            P("section", None, ("dp", "tensor")), vector, vector, up_out, vector,
            down_in, down_in, up_out,
        ),
        check_vma=False,
    )
```

```python
import functools

import jax
import jax.numpy as jnp
from jax import lax
from jax.experimental import pallas as pl
from jax.experimental.layout import Layout, with_layout_constraint
from jax.experimental.pallas import tpu as pltpu
from jax.sharding import PartitionSpec as P

HEADS = 4
KDIM = 128
VDIM = 256
RANK = 16
SUB = 16
PACK = 128
STATE_PAD = 16

norm_eps = 1e-06
head_eps = 1e-05
f32 = jnp.float32
bf16 = jnp.bfloat16
INTERPRET = False


def row_major(block):
    return with_layout_constraint(block, Layout(major_to_minor=tuple(range(block.ndim))))


def swap(block, axis):
    return lax.ppermute(block, axis, [(0, 1), (1, 0)])


def mm(left, right, dims):
    return lax.dot_general(left, right, (dims, ((), ())), preferred_element_type=f32)


def exact(left, right, dims=((1,), (0,))):
    return lax.dot_general(
        left, right, (dims, ((), ())), precision=lax.Precision.HIGHEST, preferred_element_type=f32
    )


NN = ((1,), (0,))
NT = ((1,), (1,))
TN = ((0,), (0,))


def call(body, outs, *args):
    return pl.pallas_call(
        body,
        out_shape=[jax.ShapeDtypeStruct(shape, kind) for shape, kind in outs],
        interpret=INTERPRET,
    )(*args)


def iota2(rows, cols, axis):
    return lax.broadcasted_iota(jnp.int32, (rows, cols), axis)


def lower(count):
    return jnp.where(iota2(count, count, 0) >= iota2(count, count, 1), 1.0, 0.0)


def levels(count):
    half, out = count // 2, []
    while half >= SUB:
        out.append(half)
        half //= 2
    return out


def level_factors(sums, half):
    count, width = sums.shape
    parts = sums.reshape(count // (2 * half), 2 * half, width)
    middle = jnp.broadcast_to(parts[:, half - 1 : half, :], parts.shape).reshape(count, width)
    late = (iota2(count, width, 0) & half) != 0
    gap = sums - middle
    to_late = jnp.where(late, jnp.exp(jnp.minimum(gap, 0.0)), 0.0)
    to_early = jnp.where(late, 0.0, jnp.exp(jnp.minimum(-gap, 0.0)))
    return to_late, to_early


def level_mask(count, half):
    rows, cols = iota2(count, count, 0), iota2(count, count, 1)
    bits = 2 * half - 1
    return (rows & ~bits) == (cols & ~bits)


def pair_mask(seg_col, seg_row, count):
    same = seg_col == seg_row
    return same & (iota2(count, count, 0) >= iota2(count, count, 1))


def pick_mask(count, offset):
    rows, cols = iota2(count, count, 0), iota2(count, count, 1)
    return cols == ((rows & ~(SUB - 1)) + offset)


def sub_factor(sums3, offset):
    return jnp.exp(jnp.minimum(sums3 - sums3[:, offset : offset + 1, :], 0.0))


def pre_body(
    proj, up3, bias, seg_col, seg_before, logits_o, sums_o, open_o, keep_o, end_o, through_o, pack_o
):
    count = proj.shape[0]
    logits = exact(proj[:, 768:896], up3[...]) + bias[...]
    decay = (jnp.minimum(logits, 0.0) - jnp.log1p(jnp.exp(-jnp.abs(logits)))) / 16.0
    sums = exact(lower(count), decay)
    last = sums[count - 1 : count, :]
    seg = seg_col[...]
    seg_last = seg[count - 1 : count, :]
    before = seg_before[...]
    opened = jnp.where(seg == before, proj[:, 0:128] * jnp.exp(sums), 0.0)
    kept = jnp.where(seg == seg_last, proj[:, 128:256] * jnp.exp(last - sums), 0.0)
    state = exact(proj[:, 256:512], kept, TN)
    through = jnp.where(before == seg_last, jnp.exp(last), 0.0)
    logits_o[...] = logits
    sums_o[...] = sums
    open_o[...] = opened
    keep_o[...] = kept
    end_o[...] = state
    through_o[...] = through
    pack_o[0:VDIM, :] = state.astype(bf16)
    pack_o[VDIM : VDIM + STATE_PAD, :] = jnp.broadcast_to(through, (STATE_PAD, KDIM)).astype(bf16)


def within_body(proj, sums_r, seg_col, seg_row, scores_o, out_o):
    count = proj.shape[0]
    query, key = proj[:, 0:128], proj[:, 128:256]
    sums = sums_r[...]
    scores = jnp.zeros((count, count), f32)
    for half in levels(count):
        to_late, to_early = level_factors(sums, half)
        part = exact(query * to_late, key * to_early, NT)
        scores = scores + jnp.where(level_mask(count, half), part, 0.0)
    blocks = (count // SUB, SUB, KDIM)
    query3, key3, sums3 = query.reshape(blocks), key.reshape(blocks), sums.reshape(blocks)
    for offset in range(SUB):
        weight = sub_factor(sums3, offset)
        column = jnp.sum(query3 * weight * key3[:, offset : offset + 1, :], axis=-1, keepdims=True)
        scores = jnp.where(pick_mask(count, offset), column.reshape(count, 1), scores)
    scores = jnp.where(pair_mask(seg_col[...], seg_row[...], count), scores, 0.0)
    scores_o[...] = scores
    out_o[...] = exact(scores, proj[:, 256:512])


def post_body(within, opened, state_in, proj, gain, unit_o, scale_o, branch_o):
    mixed = within[...] + exact(opened[...], state_in[...], NT)
    scale = lax.rsqrt(jnp.mean(mixed * mixed, axis=-1, keepdims=True) + head_eps)
    unit = mixed * scale
    gate = proj[:, 512:768]
    unit_o[...] = unit
    scale_o[...] = scale
    branch_o[...] = (unit * gain[...] * (gate * jax.nn.sigmoid(gate))).astype(bf16)


def head_back_body(
    branch_delta, unit_r, scale, proj, gain_r, opened, through, low_o, gain_o, mixed_o, pack_o
):
    delta, unit, gate, gain = branch_delta[...], unit_r[...], proj[:, 512:768], gain_r[...]
    sigma = jax.nn.sigmoid(gate)
    swish = gate * sigma
    slope = sigma * (1.0 + gate * (1.0 - sigma))
    low_o[...] = (delta * unit * gain * slope).astype(bf16)
    through_unit = delta * swish
    gain_o[...] = jnp.sum(through_unit * unit, axis=0, keepdims=True)
    inner = through_unit * gain
    mixed = scale[...] * (inner - unit * jnp.mean(inner * unit, axis=-1, keepdims=True))
    mixed_o[...] = mixed
    pack_o[0:VDIM, :] = exact(mixed, opened[...], TN).astype(bf16)
    pack_o[VDIM : VDIM + STATE_PAD, :] = jnp.broadcast_to(
        through[...], (STATE_PAD, KDIM)
    ).astype(bf16)


def within_back_body(
    mixed_r, proj, sums_r, scores, seg_col, seg_row, seg_before, state_in, query_o, key_o, value_o
):
    count = proj.shape[0]
    query, key, value = proj[:, 0:128], proj[:, 128:256], proj[:, 256:512]
    sums, mixed = sums_r[...], mixed_r[...]
    value_o[...] = exact(scores[...], mixed, TN)
    grad = jnp.where(
        pair_mask(seg_col[...], seg_row[...], count), exact(mixed, value, NT), 0.0
    )
    query_delta = jnp.where(
        seg_col[...] == seg_before[...], jnp.exp(sums) * exact(mixed, state_in[...]), 0.0
    )
    key_delta = jnp.zeros((count, KDIM), f32)
    for half in levels(count):
        to_late, to_early = level_factors(sums, half)
        part = jnp.where(level_mask(count, half), grad, 0.0)
        query_delta = query_delta + to_late * exact(part, key * to_early)
        key_delta = key_delta + to_early * exact(part, query * to_late, TN)
    blocks = (count // SUB, SUB, KDIM)
    query3, key3, sums3 = query.reshape(blocks), key.reshape(blocks), sums.reshape(blocks)
    place = lax.broadcasted_iota(jnp.int32, blocks, 1)
    query_sub, key_sub = jnp.zeros(blocks, f32), jnp.zeros(blocks, f32)
    for offset in range(SUB):
        weight = sub_factor(sums3, offset)
        column = jnp.sum(jnp.where(pick_mask(count, offset), grad, 0.0), axis=-1, keepdims=True)
        weighted = weight * column.reshape(count // SUB, SUB, 1)
        query_sub = query_sub + weighted * key3[:, offset : offset + 1, :]
        total = jnp.sum(weighted * query3, axis=1, keepdims=True)
        key_sub = jnp.where(place == offset, total, key_sub)
    query_o[...] = query_delta + query_sub.reshape(count, KDIM)
    key_o[...] = key_delta + key_sub.reshape(count, KDIM)


def state_back_body(
    query_d, key_d, value_d, state_grad, state_in, state_end, through, proj, sums_r, kept,
    logits, seg_col, up3, gate_low, low_o, up_o, bias_o,
):
    count = proj.shape[0]
    grad, sums = state_grad[...], sums_r[...]
    last = sums[count - 1 : count, :]
    seg = seg_col[...]
    query_delta = query_d[...]
    value_delta = value_d[...] + exact(kept[...], grad, NT)
    key_delta = key_d[...] + jnp.where(
        seg == seg[count - 1 : count, :],
        jnp.exp(last - sums) * exact(proj[:, 256:512], grad),
        0.0,
    )
    final = state_end[...] + through[...] * state_in[...]
    beyond = jnp.sum(final * grad, axis=0, keepdims=True)
    local = proj[:, 0:128] * query_delta - proj[:, 128:256] * key_delta
    decay_delta = exact(lower(count), local, TN) + beyond
    logit_delta = decay_delta * jax.nn.sigmoid(-logits[...]) / 16.0
    bias_o[...] = jnp.sum(logit_delta, axis=0, keepdims=True)
    ranks = exact(proj[:, 768:896], logit_delta, TN)
    up_o[...] = ranks[0:16, :] + ranks[16:32, :] + ranks[32:48, :]
    low_o[:, 0:128] = query_delta.astype(bf16)
    low_o[:, 128:256] = key_delta.astype(bf16)
    low_o[:, 256:512] = value_delta.astype(bf16)
    low_o[:, 512:768] = gate_low[...]
    low_o[:, 768:896] = exact(logit_delta, up3[...], NT).astype(bf16)


def scan_states(pack, backward):
    count = lax.axis_size("dp")
    here = lax.axis_index("dp")
    state = pack[:VDIM].astype(f32)
    through = pack[VDIM : VDIM + 1].astype(f32)
    carried, passed = jnp.zeros_like(state), jnp.ones_like(through)
    step = 1
    while step < count:
        other = lax.ppermute(pack, "dp", [(i, i ^ step) for i in range(count)])
        other_state = other[:VDIM].astype(f32)
        other_through = other[VDIM : VDIM + 1].astype(f32)
        mine_later = (here & step) != 0
        ahead = jnp.logical_not(mine_later) if backward else mine_later
        carried = jnp.where(ahead, carried + passed * other_state, carried)
        passed = jnp.where(ahead, passed * other_through, passed)
        state = jnp.where(ahead, state + through * other_state, other_state + other_through * state)
        through = through * other_through
        step *= 2
        if step < count:
            pack = jnp.concatenate(
                [state, jnp.broadcast_to(through, (STATE_PAD, KDIM))], axis=0
            ).astype(bf16)
    return carried


def steps_of(count):
    return [1 << k for k in range(count.bit_length() - 1)]


def butterfly_gather(block, order):
    count, here = lax.axis_size("dp"), lax.axis_index("dp")
    whole, done = block, []
    for step in order:
        other = lax.ppermute(row_major(whole), "dp", [(i, i ^ step) for i in range(count)])
        axis = sum(earlier > step for earlier in done)
        late = (here & step) != 0
        whole = jnp.stack(
            [jnp.where(late, other, whole), jnp.where(late, whole, other)], axis=axis
        )
        done.append(step)
    return whole.reshape(count * block.shape[0], block.shape[1])


def butterfly_scatter(grad, order):
    count, here = lax.axis_size("dp"), lax.axis_index("dp")
    left = sorted(order, reverse=True)
    parts = grad.reshape([2] * len(left) + [grad.shape[0] // count, grad.shape[1]])
    for step in order:
        axis = left.index(step)
        low, high = (lax.index_in_dim(parts, k, axis, keepdims=False) for k in range(2))
        late = (here & step) != 0
        send = row_major(jnp.where(late, low, high))
        got = row_major(lax.ppermute(send, "dp", [(i, i ^ step) for i in range(count)]))
        parts = (jnp.where(late, high, low).astype(f32) + got.astype(f32)).astype(bf16)
        left.remove(step)
    return parts


def gather_tokens(block, tensor_index, section_index):
    other = swap(block, "tensor")
    first = tensor_index == 0
    pair = jnp.stack([jnp.where(first, block, other), jnp.where(first, other, block)])
    far = swap(pair, "section")
    left = section_index == 0
    whole = jnp.stack([jnp.where(left, pair, far), jnp.where(left, far, pair)], axis=1)
    return whole.reshape(4 * block.shape[0], block.shape[1])


def scatter_tokens(partial, kind, tensor_index, section_index):
    rows = partial.shape[0] // 4
    parts = partial.reshape(2, 2, rows, partial.shape[1])
    left = section_index == 0
    keep = jnp.where(left, parts[:, 0], parts[:, 1])
    send = jnp.where(left, parts[:, 1], parts[:, 0])
    both = keep + swap(send, "section")
    first = tensor_index == 0
    mine = jnp.where(first, both[0], both[1])
    theirs = jnp.where(first, both[1], both[0]).astype(kind)
    return mine + swap(theirs, "tensor").astype(f32)


def rms_scale(values, epsilon):
    return lax.rsqrt(jnp.mean(values * values, axis=-1, keepdims=True) + epsilon)


def norm_back(grad_unit, unit_values, scale_values):
    return scale_values * (
        grad_unit - unit_values * jnp.mean(grad_unit * unit_values, axis=-1, keepdims=True)
    )


def layer_forward(layer_in, seg, params, where):
    attn, feed, small = params
    mixer_gain, feed_gain, up3, bias, head_gain = small
    seg_col, seg_row, seg_before = seg
    count = seg_col.shape[0]
    scale_one = rms_scale(layer_in, norm_eps)
    hidden_one = gather_tokens((layer_in * scale_one * mixer_gain).astype(bf16), *where)
    proj = mm(hidden_one, attn[:, :896], NN)
    wide, tall = (count, KDIM), (count, VDIM)
    logits, sums, opened, kept, state_end, through, pack = call(
        pre_body,
        [(wide, f32)] * 4
        + [((VDIM, KDIM), f32), ((1, KDIM), f32), ((VDIM + STATE_PAD, KDIM), bf16)],
        proj, up3, bias, seg_col, seg_before,
    )
    scores, within = call(
        within_body, [((count, count), f32), (tall, f32)], proj, sums, seg_col, seg_row
    )
    state_in = scan_states(pack, False)
    unit, scale_head, branch = call(
        post_body,
        [(tall, f32), ((count, 1), f32), (tall, bf16)],
        within, opened, state_in, proj, head_gain,
    )
    mid = layer_in + scatter_tokens(mm(branch, attn[:, 896:], NT), f32, *where)
    scale_two = rms_scale(mid, norm_eps)
    hidden_two = gather_tokens((mid * scale_two * feed_gain).astype(bf16), *where)
    units = feed.shape[1] // 3
    both = mm(hidden_two, feed[:, : 2 * units], NN)
    gate_pre, up_pre = both[:, :units], both[:, units:]
    inner = (jax.nn.silu(gate_pre) * up_pre).astype(bf16)
    result = mid + scatter_tokens(mm(inner, feed[:, 2 * units :], NT), f32, *where)
    saved = (
        layer_in, scale_one, hidden_one, proj, logits, sums, opened, kept, state_end, through,
        scores, state_in, unit, scale_head, branch, mid, scale_two, hidden_two, both, inner,
    )
    return result, saved


def scattered(grad):
    return lax.psum_scatter(grad, "dp", scatter_dimension=0, tiled=True)


def layer_backward(saved, cotangent, seg, params, where, pending, earlier):
    attn, feed, small = params
    mixer_gain, feed_gain, up3, bias, head_gain = small
    seg_col, seg_row, seg_before = seg
    (
        layer_in, scale_one, hidden_one, proj, logits, sums, opened, kept, state_end, through,
        scores, state_in, unit, scale_head, branch, mid, scale_two, hidden_two, both, inner,
    ) = saved
    count = seg_col.shape[0]
    wide, tall = (count, KDIM), (count, VDIM)
    units = feed.shape[1] // 3
    cot = gather_tokens(cotangent.astype(bf16), *where)
    inner_delta = mm(cot, feed[:, 2 * units :], NN)
    gate_pre, up_pre = both[:, :units], both[:, units:]
    sigma = jax.nn.sigmoid(gate_pre)
    gate_delta = inner_delta * up_pre * (sigma * (1.0 + gate_pre * (1.0 - sigma)))
    up_delta = inner_delta * (gate_pre * sigma)
    low_two = jnp.concatenate([gate_delta, up_delta], axis=1).astype(bf16)
    two_delta = mm(low_two, feed[:, : 2 * units], NT)
    feed_grad = jnp.concatenate(
        pending + [mm(hidden_two, low_two, TN).astype(bf16), mm(cot, inner, TN).astype(bf16)],
        axis=1,
    )
    feed_gain_grad = jnp.sum(two_delta * hidden_two.astype(f32), axis=0) / feed_gain
    two_local = scatter_tokens(two_delta, bf16, *where)
    mid_delta = cotangent + norm_back(two_local * feed_gain, mid * scale_two, scale_two)
    mid_delta, feed_grad = lax.optimization_barrier((mid_delta, feed_grad))
    feed_reduced = scattered(feed_grad)
    mid_low = gather_tokens(mid_delta.astype(bf16), *where)
    branch_delta = mm(mid_low, attn[:, 896:], NN)
    gate_low, head_gain_grad, mixed_delta, pack = call(
        head_back_body,
        [(tall, bf16), ((1, VDIM), f32), (tall, f32), ((VDIM + STATE_PAD, KDIM), bf16)],
        branch_delta, unit, scale_head, proj, head_gain, opened, through,
    )
    query_d, key_d, value_d = call(
        within_back_body,
        [(wide, f32), (wide, f32), (tall, f32)],
        mixed_delta, proj, sums, scores, seg_col, seg_row, seg_before, state_in,
    )
    out_grad = mm(mid_low, branch, TN).astype(bf16)
    state_grad = scan_states(pack, True)
    low_one, up_grad, bias_grad = call(
        state_back_body,
        [((count, 896), bf16), ((RANK, KDIM), f32), ((1, KDIM), f32)],
        query_d, key_d, value_d, state_grad, state_in, state_end, through, proj, sums, kept,
        logits, seg_col, up3, gate_low,
    )
    low_one, earlier = lax.optimization_barrier((low_one, earlier))
    one_delta = mm(low_one, attn[:, :896], NT)
    main_grad = mm(hidden_one, low_one, TN)
    mixer_gain_grad = jnp.sum(one_delta * hidden_one.astype(f32), axis=0) / mixer_gain
    depth = main_grad.shape[0]
    tensor_index, section_index = where
    head = tensor_index * 2 + section_index
    ranks = jnp.concatenate([up_grad.T, bias_grad.T, jnp.zeros((KDIM, 1), f32)], axis=1)
    ranks = lax.dynamic_update_slice(
        jnp.zeros((HEADS * KDIM, RANK + 2), f32), ranks, (head * KDIM, 0)
    ).reshape(depth, -1)
    repeat = depth // VDIM
    gains = jnp.broadcast_to(head_gain_grad.reshape(VDIM, 1), (VDIM, repeat)).reshape(depth, 1)
    smalls = jnp.concatenate(
        [main_grad[:, 768:784], mixer_gain_grad[:, None], feed_gain_grad[:, None], ranks, gains],
        axis=1,
    )
    smalls = jnp.pad(smalls, ((0, 0), (0, PACK - smalls.shape[1])))
    attn_grad = (
        main_grad[:, :768].astype(bf16),
        jnp.concatenate([smalls.astype(bf16), out_grad], axis=1),
    )
    one_local = scatter_tokens(one_delta, bf16, *where)
    input_delta = mid_delta + norm_back(one_local * mixer_gain, layer_in * scale_one, scale_one)
    if not earlier:
        input_delta, attn_grad = lax.optimization_barrier((input_delta, attn_grad))
    return input_delta, attn_grad, feed_reduced, earlier


def in_three(values):
    high = lax.reduce_precision(values, 8, 7)
    rest = values - high
    middle = lax.reduce_precision(rest, 8, 7)
    return [high.astype(bf16), middle.astype(bf16), (rest - middle).astype(bf16)]


def small_params(attn, tensor_index, section_index):
    depth = attn.shape[0]
    pack = attn[:, 768:896].astype(f32)
    rest = pack[:, 48:60] + pack[:, 60:72] + pack[:, 72:84]
    ranks = rest[:, 2:11].reshape(HEADS * KDIM, RANK + 2)
    head = tensor_index * 2 + section_index
    ranks = lax.dynamic_slice_in_dim(ranks, head * KDIM, KDIM, 0).T
    up = ranks[:RANK]
    up3 = jnp.concatenate([up, up, up, jnp.zeros((PACK - 3 * RANK, KDIM), f32)], axis=0)
    head_gain = rest[:, 11].reshape(VDIM, depth // VDIM)[:, 0]
    return rest[:, 0], rest[:, 1], up3, ranks[RANK : RANK + 1], head_gain[None]


def shards(
    inputs, segments, mixer_gain, query_weight, key_weight, value_weight, outgate_weight,
    decay_down, decay_up, decay_bias, head_gain, output_weight, feed_gain, gate_weight,
    up_weight, down_weight, cotangent,
):
    section_index = lax.axis_index("section")
    tensor_index = lax.axis_index("tensor")
    dp_index = lax.axis_index("dp")
    where = (tensor_index, section_index)
    left, first = section_index == 0, tensor_index == 0
    segment_ids = segments.astype(f32)
    count = segment_ids.shape[0]

    narrow = mixer_gain.shape[1]
    ranks = jnp.concatenate(
        [decay_up[0].T, decay_bias[0][:, None], jnp.zeros((decay_bias.shape[1], 1), f32)], axis=1
    ).reshape(narrow, -1)
    spread = narrow // head_gain.shape[1]
    gains = jnp.broadcast_to(head_gain[0][:, None], (head_gain.shape[1], spread)).reshape(narrow, 1)
    mine = jnp.concatenate(
        [decay_down[0], mixer_gain[0][:, None], feed_gain[0][:, None], ranks, gains], axis=1
    )
    theirs = swap(mine, "tensor")
    rows = jnp.concatenate([jnp.where(first, mine, theirs), jnp.where(first, theirs, mine)], axis=0)
    seg_end = jnp.broadcast_to(segment_ids[-1:][None], (2 * narrow, 1)).astype(bf16)
    pack = jnp.concatenate(in_three(rows[:, :RANK]) + in_three(rows[:, RANK:]) + [seg_end], axis=1)
    pack = jnp.pad(pack, ((0, 0), (0, PACK - pack.shape[1])))

    def half(weight, side):
        width = weight.shape[1] // 2
        return weight[:, side * width : (side + 1) * width]

    out_t, down_t = output_weight[0].T, down_weight[0].T

    def attn_half(side):
        parts = [half(w, side) for w in (query_weight[0], key_weight[0], value_weight[0], outgate_weight[0])]
        return jnp.concatenate(parts + [pack, half(out_t, side)], axis=1)

    def feed_half(side):
        parts = [half(w, side) for w in (gate_weight[0], up_weight[0], down_t)]
        return jnp.concatenate(parts, axis=1)

    def per_layer(side_zero, side_one):
        keep = jnp.where(left, side_zero, side_one)
        got = row_major(swap(row_major(jnp.where(left, side_one, side_zero)), "section"))
        return jnp.where(left, keep, got), jnp.where(left, got, keep)

    attn_parts = per_layer(attn_half(0), attn_half(1))
    feed_parts = per_layer(feed_half(0), feed_half(1))

    def gathered(part):
        return lax.all_gather(row_major(part), "dp", axis=0, tiled=True)

    attn_width = attn_parts[0].shape[1]
    near_first = steps_of(lax.axis_size("dp"))
    far_first = near_first[::-1]
    cut = 640
    attn0 = jnp.concatenate(
        [
            butterfly_gather(attn_parts[0][:, :cut], far_first),
            butterfly_gather(attn_parts[0][:, cut:], near_first),
        ],
        axis=1,
    )
    middle = gathered(jnp.concatenate([attn_parts[1], feed_parts[0]], axis=1))
    feed1 = gathered(feed_parts[1])
    wide = 2 * narrow
    earlier = lax.dynamic_slice(
        attn0, (jnp.maximum(dp_index - 1, 0) * wide, 768 + 84), (1, 1)
    ).astype(f32)
    seg_before = jnp.where(dp_index == 0, -1.0, earlier)
    seg = (segment_ids[:, None], segment_ids[None, :], seg_before)

    own = inputs.shape[0] // 2
    layer_in = lax.dynamic_slice_in_dim(inputs, section_index * own, own, 0)
    cot = lax.dynamic_slice_in_dim(cotangent, section_index * own, own, 0)
    params0 = (attn0, middle[:, attn_width:], small_params(attn0, *where))
    out0, saved0 = layer_forward(layer_in, seg, params0, where)
    late, out0 = lax.optimization_barrier((middle, out0))
    attn1 = late[:, :attn_width]
    params1 = (attn1, feed1, small_params(attn1, *where))
    out1, saved1 = layer_forward(out0, seg, params1, where)
    delta1, attn_grad1, feed_red1, _ = layer_backward(saved1, cot, seg, params1, where, [], [])
    delta0, attn_grad0, mixed_red, (feed_red1,) = layer_backward(
        saved0, delta1, seg, params0, where, list(attn_grad1), [feed_red1]
    )
    attn_red0 = jnp.concatenate(
        [
            butterfly_scatter(attn_grad0[0], near_first),
            butterfly_scatter(attn_grad0[1], far_first),
        ],
        axis=1,
    )
    mixed_red, attn_red0 = lax.optimization_barrier((mixed_red, attn_red0))
    attn_red1, feed_red0 = mixed_red[:, :attn_width], mixed_red[:, attn_width:]

    def to_section(of_zero, of_one):
        keep = jnp.where(left, of_zero, of_one)
        got = swap(jnp.where(left, of_one, of_zero), "section")
        return keep, got

    def joined(keep, got, axis):
        return jnp.concatenate([jnp.where(left, keep, got), jnp.where(left, got, keep)], axis=axis)

    section_out = joined(*to_section(out0, out1), 0)
    input_grad = joined(*to_section(delta0, delta1), 0)
    attn_keep, attn_got = to_section(attn_red0, attn_red1)
    feed_keep, feed_got = to_section(feed_red0, feed_red1)

    def columns(keep, got, start, width):
        return joined(keep[:, start : start + width], got[:, start : start + width], 1).astype(f32)

    units = feed_keep.shape[1] // 3
    small = attn_keep[:, 768:896].astype(f32) + attn_got[:, 768:896].astype(f32)
    small_mine = jnp.where(first, small[:narrow], small[narrow:])
    small_theirs = jnp.where(first, small[narrow:], small[:narrow])
    small = small_mine + swap(small_theirs, "tensor")
    ranks = small[:, 18:27].reshape(decay_bias.shape[1], RANK + 2)
    outs = (
        section_out,
        input_grad,
        small[:, 16],
        columns(attn_keep, attn_got, 0, 128),
        columns(attn_keep, attn_got, 128, 128),
        columns(attn_keep, attn_got, 256, 256),
        columns(attn_keep, attn_got, 512, 256),
        small[:, :16],
        ranks[:, :RANK].T,
        ranks[:, RANK],
        small[:, 27].reshape(-1, spread)[:, 0],
        columns(attn_keep, attn_got, 896, 256).T,
        small[:, 17],
        columns(feed_keep, feed_got, 0, units),
        columns(feed_keep, feed_got, units, units),
        columns(feed_keep, feed_got, 2 * units, units).T,
    )
    return tuple(out[None] for out in outs)


def solution(mesh):
    rows = P(("dp", "tensor"), None)
    vector = P("section", ("dp", "tensor"))
    down_in = P("section", "dp", "tensor")
    up_out = P("section", "tensor", "dp")
    placed = (
        rows, P("dp"), vector, down_in, down_in, down_in, down_in,
        P("section", ("dp", "tensor"), None), P("section", None, ("dp", "tensor")),
        vector, vector, up_out, vector, down_in, down_in, up_out, rows,
    )
    tokens = P("section", ("dp", "tensor"), None)
    return jax.shard_map(
        shards,
        mesh=mesh,
        in_specs=placed,
        out_specs=(
            tokens, tokens, vector, down_in, down_in, down_in, down_in, tokens,
            P("section", None, ("dp", "tensor")), vector, vector, up_out, vector,
            down_in, down_in, up_out,
        ),
        check_vma=False,
    )
```
